512 devices in a mesh: vec: 64 (over x, z_hi, y), orb: 8 (over z_lo, core).
Axes of the slice: x: 4, y: 4, z: 16 (z_hi: 4, z_lo: 4; z = z_hi * 4 + z_lo), core: 2. Of those that a mesh axis runs over, the one named last changes fastest.
Arguments:
- cholesky: bfloat16 [256, 2048, 2048], P('vec', 'orb'), may hold values from -4 to 4
- active_coeff: bfloat16 [2048, 24], replicated, may hold values from -0.125 to 0.125
- pair_density: bfloat16 [24, 24, 576], replicated, may hold values from -0.0546875 to 0.0546875
Outputs:
- active_integrals: float32 [2048, 24, 576], P(('orb', 'vec'))
- general_fock: float32 [2048, 24], P(('orb', 'vec'))
The draws below stay inside these ranges and needn't reach their ends.
All inputs are finite; a program needn't handle non-finite values.
Results may differ from the reference program's by a relative error of at most 0.0049.
Values may be sent and summed in bfloat16 or wider, within the bound.
A program may use at most 64 MiB of HBM per device.

```python
import jax
import jax.numpy as jnp
from jax import lax

NB = 2048
NA = 24
NQ = 256


def block_scale(own_key, shape, pieces, least, largest):
    factor_of = 1.0
    for axis_at, parts in pieces:
        draws = jax.random.uniform(jax.random.fold_in(jax.random.fold_in(own_key, 6), axis_at), (parts,), jnp.float32, least / len(pieces), largest / len(pieces))
        factor_of = factor_of * jnp.repeat(jnp.exp(draws), shape[axis_at] // parts).reshape((-1,) + (1,) * (len(shape) - 1 - axis_at))
    return factor_of


def bell_draw(key, shape, width, most, pieces=(), dtype=jnp.bfloat16):
    array = width * jax.random.normal(key, shape, jnp.float32)
    if pieces:
        array = array * block_scale(key, shape, pieces, -0.22, 0.18)
    return jnp.clip(array, -most, most).astype(dtype)


def setup_inputs(seed: int = 0) -> dict:
    key_of = jax.random.split(jax.random.key(seed), 4)
    cholesky = bell_draw(key_of[0], (NQ, NB, NB), 0.25, 4.0, ((0, 64), (1, 8)))
    active_coeff = bell_draw(key_of[1], (NB, NA), NB ** -0.5, 0.125)
    pair_density = bell_draw(key_of[2], (NA, NA, NA * NA), (NA * NA * NA) ** -0.5, 0.0546875)
    return {"cholesky": cholesky, "active_coeff": active_coeff, "pair_density": pair_density}


def reference(cholesky, active_coeff, pair_density):
    coeff_wide = active_coeff.astype(jnp.float32)

    def transform(vector):
        return jnp.dot(vector.astype(jnp.float32), coeff_wide, precision=lax.Precision.HIGHEST)

    half = lax.map(transform, cholesky).astype(jnp.bfloat16)
    half_wide = half.astype(jnp.float32)
    active_sum = jnp.einsum("mv,qmw->qvw", coeff_wide, half_wide, precision=lax.Precision.HIGHEST)
    active = active_sum.reshape(NQ, NA * NA).astype(jnp.bfloat16)
    active_wide = active.astype(jnp.float32)
    integrals = jnp.einsum("qmu,qx->mux", half_wide, active_wide, precision=lax.Precision.HIGHEST)
    density = pair_density.astype(jnp.float32).reshape(NA, NA * NA * NA)
    fock = jnp.dot(integrals.reshape(NB, NA * NA * NA), density.T, precision=lax.Precision.HIGHEST)
    return integrals, fock
```

```python
import jax
import jax.numpy as jnp
from jax import lax
from jax.experimental import pallas as pl
from jax.experimental.pallas import tpu as pltpu
from jax.sharding import PartitionSpec as P

MESH = pl.DeviceIdType.MESH
F32 = jnp.float32
BF16 = jnp.bfloat16
NT = (((1,), (1,)), ((), ()))
TN = (((0,), (0,)), ((), ()))


def kernel(
    chol, coeff_t, density, out, fock,
    chol_v, coeff_pad, coeff_blk, density_v, half32, spread, rows_out, rows_in, rows32,
    turn_out, turn_in, turn32, part32, pair_in, part_out, part_in, sum32, block_out, gathered, ints,
    chol_sem, density_sem, pair_send, pair_recv, rows_send, rows_recv, part_send, part_recv,
    turn_send, turn_recv, block_send, block_recv, share_send, share_recv,
):
    vec, orb = lax.axis_index("vec"), lax.axis_index("orb")
    x, zh, y = vec // 16, (vec // 4) % 4, vec % 4
    zl, core = orb // 2, orb % 2

    def plane(k):
        return (((x + k // 4) % 4) * 16 + zh * 4 + (y + k % 4) % 4, orb)

    def column(k):
        return (x * 16 + ((zh + k // 4) % 4) * 4 + y, ((zl + k % 4) % 4) * 2 + core)

    sibling = (vec, zl * 2 + 1 - core)

    def remote(src, dst, send, recv, device):
        return pltpu.make_async_remote_copy(
            src_ref=src, dst_ref=dst, send_sem=send, recv_sem=recv, device_id=device, device_id_type=MESH
        )

    barrier = pltpu.get_barrier_semaphore()
    pl.semaphore_signal(barrier, inc=1, device_id=sibling, device_id_type=MESH)

    @pl.loop(1, 16)
    def _(k):
        pl.semaphore_signal(barrier, inc=1, device_id=column(k), device_id_type=MESH)
        pl.semaphore_signal(barrier, inc=1, device_id=plane(k), device_id_type=MESH)

    def fetch(n):
        piece = (n // 2, pl.ds((n % 2) * 128, 128))
        return pltpu.make_async_copy(chol.at[piece], chol_v.at[piece], chol_sem.at[n])

    for n in range(8):
        fetch(n).start()
    density_copy = pltpu.make_async_copy(density, density_v, density_sem)
    density_copy.start()

    coeff_pad[...] = jnp.zeros_like(coeff_pad)
    coeff_pad[0:24, :] = coeff_t[...]
    for n in range(2):
        lanes = pl.ds(pl.multiple_of(orb * 256 + n * 128, 128), 128)
        coeff_blk[n * 24 : n * 24 + 24, :] = coeff_t[:, lanes].astype(F32)
    coeff_rows = jnp.concatenate(
        [
            jnp.concatenate([coeff_blk[pl.ds(n * 24 + k, 8, stride=3), :] for k in range(3)], axis=0)
            for n in range(2)
        ],
        axis=1,
    ).astype(BF16)

    for q in range(4):
        for n in range(2):
            fetch(2 * q + n).wait()
            rows = lax.dot_general(
                chol_v[q, n * 128 : n * 128 + 128, :], coeff_pad[...], NT, preferred_element_type=F32
            )
            half32[q * 256 + n * 128 : q * 256 + n * 128 + 128, :] = rows.astype(BF16).astype(F32)
        part = jnp.dot(
            coeff_rows, half32[q * 256 : q * 256 + 256, :].astype(BF16), preferred_element_type=F32
        )
        packed = part[0:8] + pltpu.roll(part[8:16], 24, 1) + pltpu.roll(part[16:24], 48, 1)
        part32[0, q * 4 : q * 4 + 4, :] = packed[0:4]
        part32[1, q * 4 : q * 4 + 4, :] = packed[4:8]

    pl.semaphore_wait(barrier, 31)

    pair_copy = remote(part32.at[1 - core], pair_in, pair_send, pair_recv, sibling)
    pair_copy.start()

    for yy in range(4):
        for zz in range(4):
            at = zz * 16 + yy * 4
            group = half32[pl.ds(at, 16, stride=64), :]
            for i in range(1, 4):
                group = group + pltpu.roll(half32[pl.ds(at + i, 16, stride=64), :], 24 * i, 1)
            spread[yy * 64 + zz * 16 : yy * 64 + zz * 16 + 16, :] = group
        for xx in range(4):
            rows_out[xx * 4 + yy] = spread[pl.ds(yy * 64 + xx, 16, stride=4), :].astype(BF16)

    def rows_copy(k):
        to = ((x + k // 4) % 4) * 4 + (y + k % 4) % 4
        return remote(rows_out.at[to], rows_in.at[k], rows_send.at[k], rows_recv.at[k], plane(k))

    @pl.loop(1, 16)
    def _(k):
        rows_copy(k).start()

    pair_copy.wait_recv()
    mine = (part32[core] + pair_in[...]).astype(BF16)
    part_out[...] = mine
    part_in[0] = mine

    def part_copy(k):
        return remote(part_out, part_in.at[k], part_send.at[k], part_recv.at[k], column(k))

    @pl.loop(1, 16)
    def _(k):
        part_copy(k).start()

    rows_in[0] = rows_out[x * 4 + y]

    @pl.loop(1, 16)
    def _(k):
        rows_copy(k).wait_recv()

    for k in range(16):
        rows32[k * 16 : k * 16 + 16, :] = rows_in[k].astype(F32)
    for zz in range(4):
        for q in range(4):
            turn_out[zz, q * 16 : q * 16 + 16, :] = rows32[pl.ds(zz * 4 + q, 16, stride=16), :].astype(BF16)

    def turn_copy(k):
        to = (zh + k) % 4
        device = (x * 16 + to * 4 + y, orb)
        return remote(turn_out.at[to], turn_in.at[k], turn_send.at[k], turn_recv.at[k], device)

    @pl.loop(1, 4)
    def _(k):
        turn_copy(k).start()

    turn_in[0] = turn_out[zh]

    @pl.loop(1, 16)
    def _(k):
        part_copy(k).wait_recv()

    for h in range(4):
        total = part_in[4 * h].astype(F32)
        for n in range(1, 4):
            total = total + part_in[4 * h + n].astype(F32)
        sum32[h * 16 : h * 16 + 16, :] = total
    piece = [sum32[pl.ds(j, 16, stride=4), :] for j in range(4)]
    lane = lax.broadcasted_iota(jnp.int32, (16, 128), 1)
    one, two, three = pltpu.roll(piece[1], 72, 1), pltpu.roll(piece[2], 16, 1), pltpu.roll(piece[3], 88, 1)
    left = (piece[0] + jnp.where(lane >= 72, one, 0.0)).astype(BF16)
    middle = (jnp.where(lane < 16, one, 0.0) + two + jnp.where(lane >= 88, three, 0.0)).astype(BF16)
    right = jnp.where(lane < 32, three, 0.0).astype(BF16)
    for n, tile in enumerate((left, middle, right)):
        block_out[:, n * 128 : n * 128 + 128] = tile
        gathered[core, 0, :, n * 128 : n * 128 + 128] = tile

    def block_copy(k):
        return remote(block_out, gathered.at[core, k], block_send.at[k], block_recv.at[k], plane(k))

    def share_copy(k):
        there = gathered.at[core, k]
        return remote(there, there, share_send.at[k], share_recv.at[k], sibling)

    @pl.loop(1, 16)
    def _(k):
        block_copy(k).start()

    share_copy(0).start()

    @pl.loop(1, 4)
    def _(k):
        turn_copy(k).wait_recv()

    for k in range(4):
        turn32[k * 64 : k * 64 + 64, :] = turn_in[k].astype(F32)
    own = jnp.concatenate([turn32[pl.ds(k, 16, stride=16), :] for k in range(16)], axis=0)
    own = own.astype(BF16)[:, 0:96]

    @pl.loop(1, 16)
    def _(k):
        block_copy(k).wait_recv()
        share_copy(k).start()

    @pl.loop(0, 16)
    def _(k):
        there = gathered.at[1 - core, k]
        remote(there, there, share_send.at[k], share_recv.at[k], sibling).wait_recv()

    first = lax.dot_general(own, gathered[0].reshape(256, 384), TN, preferred_element_type=F32)
    second = lax.dot_general(own, gathered[1].reshape(256, 384), TN, preferred_element_type=F32)
    lane = lax.broadcasted_iota(jnp.int32, (96, 128), 1)
    a, b, c = (pltpu.roll(second[:, n * 128 : n * 128 + 128], 32, 1) for n in range(3))
    tiles = (
        first[:, 0:128],
        first[:, 128:256],
        first[:, 256:384] + jnp.where(lane >= 32, a, 0.0),
        jnp.where(lane < 32, a, b),
        jnp.where(lane < 32, b, c),
    )
    for n, tile in enumerate(tiles):
        width = min(128, 576 - n * 128)
        tile = tile[:, 0:width]
        out[:, :, n * 128 : n * 128 + width] = tile.reshape(4, 24, width)
        high = tile.astype(BF16)
        ints[0:96, n * 128 : n * 128 + width] = high
        ints[96:192, n * 128 : n * 128 + width] = (tile - high.astype(F32)).astype(BF16)

    density_copy.wait()
    pairs = lax.dot_general(ints[...], density_v[...], NT, preferred_element_type=F32)
    pairs = pairs[0:96] + pairs[96:192]
    row = lax.broadcasted_iota(jnp.int32, (96, 576), 0) % 24
    col = lax.broadcasted_iota(jnp.int32, (96, 576), 1) % 24
    kept = jnp.where(row == col, pairs, 0.0).reshape(4, 24, 576).sum(axis=1)
    pick = lax.broadcasted_iota(jnp.int32, (576, 24), 0) // 24 == lax.broadcasted_iota(jnp.int32, (576, 24), 1)
    fock[...] = jnp.dot(kept, pick.astype(F32), precision=lax.Precision.HIGHEST, preferred_element_type=F32)

    pair_copy.wait_send()
    share_copy(0).wait_send()

    @pl.loop(1, 16)
    def _(k):
        rows_copy(k).wait_send()
        part_copy(k).wait_send()
        block_copy(k).wait_send()
        share_copy(k).wait_send()

    @pl.loop(1, 4)
    def _(k):
        turn_copy(k).wait_send()


def shards(cholesky, active_coeff, pair_density):
    vmem = pl.BlockSpec(memory_space=pltpu.VMEM)
    hbm = pl.BlockSpec(memory_space=pl.ANY)
    dma = pltpu.SemaphoreType.DMA
    return pl.pallas_call(
        kernel,
        name="half_active_fock",
        out_shape=(jax.ShapeDtypeStruct((4, 24, 576), F32), jax.ShapeDtypeStruct((4, 24), F32)),
        in_specs=[hbm, vmem, hbm],
        out_specs=(vmem, vmem),
        scratch_shapes=[
            pltpu.VMEM((4, 256, 2048), BF16),
            pltpu.VMEM((128, 2048), BF16),
            pltpu.VMEM((48, 128), F32),
            pltpu.VMEM((576, 576), BF16),
            pltpu.VMEM((1024, 128), F32),
            pltpu.VMEM((256, 128), F32),
            pltpu.VMEM((16, 16, 128), BF16),
            pltpu.VMEM((16, 16, 128), BF16),
            pltpu.VMEM((256, 128), F32),
            pltpu.VMEM((4, 64, 128), BF16),
            pltpu.VMEM((4, 64, 128), BF16),
            pltpu.VMEM((256, 128), F32),
            pltpu.VMEM((2, 16, 128), F32),
            pltpu.VMEM((16, 128), F32),
            pltpu.VMEM((16, 128), BF16),
            pltpu.VMEM((16, 16, 128), BF16),
            pltpu.VMEM((64, 128), F32),
            pltpu.VMEM((16, 384), BF16),
            pltpu.VMEM((2, 16, 16, 384), BF16),
            pltpu.VMEM((192, 576), BF16),
            dma((8,)), dma, dma, dma, dma((16,)), dma((16,)), dma((16,)), dma((16,)),
            dma((4,)), dma((4,)), dma((16,)), dma((16,)), dma((16,)), dma((16,)),
        ],
        compiler_params=pltpu.CompilerParams(
            collective_id=0, has_side_effects=True, vmem_limit_bytes=32 * 2**20
        ),
    )(cholesky, active_coeff.T, pair_density.reshape(576, 576))


def solution(mesh):
    return jax.shard_map(
        shards,
        mesh=mesh,
        in_specs=(P("vec", "orb", None), P(), P()),
        out_specs=(P(("orb", "vec"), None, None), P(("orb", "vec"), None)),
        check_vma=False,
    )
```

```python
import jax
import jax.numpy as jnp
from jax import lax
from jax.experimental import pallas as pl
from jax.experimental.pallas import tpu as pltpu
from jax.sharding import PartitionSpec as P

MESH = pl.DeviceIdType.MESH
F32 = jnp.float32
BF16 = jnp.bfloat16
NT = (((1,), (1,)), ((), ()))
TN = (((0,), (0,)), ((), ()))


def kernel(
    chol, coeff_h, density, out, fock,
    chol_v, coeff_t, coeff_pad, coeff_blk, density_v, half32, rows_out, rows_in, rows32,
    turn_out, turn_in, part32, pair_in, part_out, part_in, sum32, block_out, gathered, ints,
    chol_sem, coeff_sem, density_sem, pair_send, pair_recv, rows_send, rows_recv, part_send, part_recv,
    turn_send, turn_recv, block_send, block_recv, share_send, share_recv,
):
    vec, orb = lax.axis_index("vec"), lax.axis_index("orb")
    x, zh, y = vec // 16, (vec // 4) % 4, vec % 4
    zl, core = orb // 2, orb % 2

    def plane(k):
        return (((x + k // 4) % 4) * 16 + zh * 4 + (y + k % 4) % 4, orb)

    def column(k):
        return (x * 16 + ((zh + k // 4) % 4) * 4 + y, ((zl + k % 4) % 4) * 2 + core)

    sibling = (vec, zl * 2 + 1 - core)

    def remote(src, dst, send, recv, device):
        return pltpu.make_async_remote_copy(
            src_ref=src, dst_ref=dst, send_sem=send, recv_sem=recv, device_id=device, device_id_type=MESH
        )

    def fetch(n):
        piece = (n // 2, pl.ds((n % 2) * 128, 128))
        return pltpu.make_async_copy(chol.at[piece], chol_v.at[piece], chol_sem.at[n])

    coeff_copy = pltpu.make_async_copy(coeff_h, coeff_t, coeff_sem)
    coeff_copy.start()
    for n in range(8):
        fetch(n).start()
    density_copy = pltpu.make_async_copy(density, density_v, density_sem)
    density_copy.start()

    barrier = pltpu.get_barrier_semaphore()
    pl.semaphore_signal(barrier, inc=1, device_id=sibling, device_id_type=MESH)

    @pl.loop(1, 16)
    def _(k):
        pl.semaphore_signal(barrier, inc=1, device_id=column(k), device_id_type=MESH)
        pl.semaphore_signal(barrier, inc=1, device_id=plane(k), device_id_type=MESH)

    coeff_pad[...] = jnp.zeros_like(coeff_pad)
    coeff_copy.wait()
    coeff_pad[0:24, :] = coeff_t[...]
    for n in range(2):
        lanes = pl.ds(pl.multiple_of(orb * 256 + n * 128, 128), 128)
        coeff_blk[n * 24 : n * 24 + 24, :] = coeff_t[:, lanes].astype(F32)
    coeff_rows = jnp.concatenate(
        [
            jnp.concatenate([coeff_blk[pl.ds(n * 24 + k, 8, stride=3), :] for k in range(3)], axis=0)
            for n in range(2)
        ],
        axis=1,
    ).astype(BF16)

    for q in range(4):
        for n in range(2):
            fetch(2 * q + n).wait()
            rows = lax.dot_general(
                chol_v[q, n * 128 : n * 128 + 128, :], coeff_pad[...], NT, preferred_element_type=F32
            )
            half32[q * 256 + n * 128 : q * 256 + n * 128 + 128, :] = rows.astype(BF16).astype(F32)
        part = jnp.dot(
            coeff_rows, half32[q * 256 : q * 256 + 256, :].astype(BF16), preferred_element_type=F32
        )
        packed = part[0:8] + pltpu.roll(part[8:16], 24, 1) + pltpu.roll(part[16:24], 48, 1)
        part32[0, q * 4 : q * 4 + 4, :] = packed[0:4]
        part32[1, q * 4 : q * 4 + 4, :] = packed[4:8]

    pl.semaphore_wait(barrier, 31)

    pair_copy = remote(part32.at[1 - core], pair_in, pair_send, pair_recv, sibling)
    pair_copy.start()

    lane = lax.broadcasted_iota(jnp.int32, (16, 128), 1)
    for zz in range(4):
        tiles = [None] * 3
        for n in range(16):
            at, shift = divmod(24 * n, 128)
            group = half32[pl.ds(zz * 16 + n, 16, stride=64), :]
            group = pltpu.roll(group, shift, 1) if shift else group
            if shift > 104:
                tiles[at + 1] = jnp.where(lane < shift, group, 0.0)
                group = jnp.where(lane >= shift, group, 0.0)
            tiles[at] = group if tiles[at] is None else tiles[at] + group
        for n in range(3):
            rows_out[zz, :, n * 128 : n * 128 + 128] = tiles[n].astype(BF16)

    def rows_copy(k):
        to = (zh + k) % 4
        device = (x * 16 + to * 4 + y, orb)
        return remote(rows_out.at[to], rows_in.at[k], rows_send.at[k], rows_recv.at[k], device)

    @pl.loop(1, 4)
    def _(k):
        rows_copy(k).start()

    pair_copy.wait_recv()
    mine = (part32[core] + pair_in[...]).astype(BF16)
    part_out[...] = mine
    part_in[0] = mine

    def part_copy(k):
        return remote(part_out, part_in.at[k], part_send.at[k], part_recv.at[k], column(k))

    @pl.loop(1, 16)
    def _(k):
        part_copy(k).start()

    rows_in[0] = rows_out[zh]

    @pl.loop(1, 4)
    def _(k):
        rows_copy(k).wait_recv()

    for k in range(4):
        for n in range(3):
            rows32[n * 64 + k * 16 : n * 64 + k * 16 + 16, :] = rows_in[k, :, n * 128 : n * 128 + 128].astype(F32)
    for xx in range(4):
        t = [rows32[pl.ds(n * 64 + xx, 16, stride=4), :] for n in range(3)]
        owners = (
            t[0],
            jnp.where(lane < 32, pltpu.roll(t[0], 32, 1), pltpu.roll(t[1], 32, 1)),
            jnp.where(lane < 64, pltpu.roll(t[1], 64, 1), pltpu.roll(t[2], 64, 1)),
            pltpu.roll(t[2], 96, 1),
        )
        for yy in range(4):
            turn_out[xx * 4 + yy] = owners[yy].astype(BF16)

    def turn_copy(k):
        to = ((x + k // 4) % 4) * 4 + (y + k % 4) % 4
        return remote(turn_out.at[to], turn_in.at[k], turn_send.at[k], turn_recv.at[k], plane(k))

    @pl.loop(1, 16)
    def _(k):
        turn_copy(k).start()

    turn_in[0] = turn_out[x * 4 + y]

    @pl.loop(1, 16)
    def _(k):
        part_copy(k).wait_recv()

    for h in range(4):
        total = part_in[4 * h].astype(F32)
        for n in range(1, 4):
            total = total + part_in[4 * h + n].astype(F32)
        sum32[h * 16 : h * 16 + 16, :] = total
    piece = [sum32[pl.ds(j, 16, stride=4), :] for j in range(4)]
    one, two, three = pltpu.roll(piece[1], 72, 1), pltpu.roll(piece[2], 16, 1), pltpu.roll(piece[3], 88, 1)
    left = (piece[0] + jnp.where(lane >= 72, one, 0.0)).astype(BF16)
    middle = (jnp.where(lane < 16, one, 0.0) + two + jnp.where(lane >= 88, three, 0.0)).astype(BF16)
    right = jnp.where(lane < 32, three, 0.0).astype(BF16)
    for n, tile in enumerate((left, middle, right)):
        block_out[:, n * 128 : n * 128 + 128] = tile
        gathered[core, 0, :, n * 128 : n * 128 + 128] = tile

    def block_copy(k):
        return remote(block_out, gathered.at[core, k], block_send.at[k], block_recv.at[k], plane(k))

    def share_copy(k):
        there = gathered.at[core, k]
        return remote(there, there, share_send.at[k], share_recv.at[k], sibling)

    @pl.loop(1, 16)
    def _(k):
        block_copy(k).start()

    share_copy(0).start()

    @pl.loop(1, 16)
    def _(k):
        block_copy(k).wait_recv()
        share_copy(k).start()

    @pl.loop(0, 16)
    def _(k):
        there = gathered.at[1 - core, k]
        remote(there, there, share_send.at[k], share_recv.at[k], sibling).wait_recv()

    @pl.loop(1, 16)
    def _(k):
        turn_copy(k).wait_recv()

    own = turn_in[...].reshape(256, 128)[:, 0:96]
    first = lax.dot_general(own, gathered[0].reshape(256, 384), TN, preferred_element_type=F32)
    second = lax.dot_general(own, gathered[1].reshape(256, 384), TN, preferred_element_type=F32)
    lane = lax.broadcasted_iota(jnp.int32, (96, 128), 1)
    a, b, c = (pltpu.roll(second[:, n * 128 : n * 128 + 128], 32, 1) for n in range(3))
    tiles = (
        first[:, 0:128],
        first[:, 128:256],
        first[:, 256:384] + jnp.where(lane >= 32, a, 0.0),
        jnp.where(lane < 32, a, b),
        jnp.where(lane < 32, b, c),
    )
    for n, tile in enumerate(tiles):
        width = min(128, 576 - n * 128)
        tile = tile[:, 0:width]
        out[:, :, n * 128 : n * 128 + width] = tile.reshape(4, 24, width)
        high = tile.astype(BF16)
        ints[0:96, n * 128 : n * 128 + width] = high
        ints[96:192, n * 128 : n * 128 + width] = (tile - high.astype(F32)).astype(BF16)

    density_copy.wait()
    pairs = lax.dot_general(ints[...], density_v[...], NT, preferred_element_type=F32)
    pairs = pairs[0:96] + pairs[96:192]
    row = lax.broadcasted_iota(jnp.int32, (96, 576), 0) % 24
    col = lax.broadcasted_iota(jnp.int32, (96, 576), 1) % 24
    kept = jnp.where(row == col, pairs, 0.0).reshape(4, 24, 576).sum(axis=1)
    pick = lax.broadcasted_iota(jnp.int32, (576, 24), 0) // 24 == lax.broadcasted_iota(jnp.int32, (576, 24), 1)
    fock[...] = jnp.dot(kept, pick.astype(F32), precision=lax.Precision.HIGHEST, preferred_element_type=F32)

    pair_copy.wait_send()
    share_copy(0).wait_send()

    @pl.loop(1, 16)
    def _(k):
        turn_copy(k).wait_send()
        part_copy(k).wait_send()
        block_copy(k).wait_send()
        share_copy(k).wait_send()

    @pl.loop(1, 4)
    def _(k):
        rows_copy(k).wait_send()


def shards(cholesky, active_coeff, pair_density):
    vmem = pl.BlockSpec(memory_space=pltpu.VMEM)
    hbm = pl.BlockSpec(memory_space=pltpu.HBM)
    dma = pltpu.SemaphoreType.DMA
    return pl.pallas_call(
        kernel,
        name="half_active_fock",
        out_shape=(jax.ShapeDtypeStruct((4, 24, 576), F32), jax.ShapeDtypeStruct((4, 24), F32)),
        in_specs=[hbm, hbm, hbm],
        out_specs=(vmem, vmem),
        scratch_shapes=[
            pltpu.VMEM((4, 256, 2048), BF16),
            pltpu.VMEM((24, 2048), BF16),
            pltpu.VMEM((128, 2048), BF16),
            pltpu.VMEM((48, 128), F32),
            pltpu.VMEM((576, 576), BF16),
            pltpu.VMEM((1024, 128), F32),
            pltpu.VMEM((4, 16, 384), BF16),
            pltpu.VMEM((4, 16, 384), BF16),
            pltpu.VMEM((192, 128), F32),
            pltpu.VMEM((16, 16, 128), BF16),
            pltpu.VMEM((16, 16, 128), BF16),
            pltpu.VMEM((2, 16, 128), F32),
            pltpu.VMEM((16, 128), F32),
            pltpu.VMEM((16, 128), BF16),
            pltpu.VMEM((16, 16, 128), BF16),
            pltpu.VMEM((64, 128), F32),
            pltpu.VMEM((16, 384), BF16),
            pltpu.VMEM((2, 16, 16, 384), BF16),
            pltpu.VMEM((192, 576), BF16),
            dma((8,)), dma, dma, dma, dma, dma((4,)), dma((4,)), dma((16,)), dma((16,)),
            dma((16,)), dma((16,)), dma((16,)), dma((16,)), dma((16,)), dma((16,)),
        ],
        compiler_params=pltpu.CompilerParams(
            collective_id=0, has_side_effects=True, vmem_limit_bytes=16 * 2**20
        ),
    )(
        *(
            pltpu.with_memory_space_constraint(array, pltpu.HBM)
            for array in (cholesky, active_coeff.T, pair_density.reshape(576, 576))
        )
    )


def solution(mesh):
    return jax.shard_map(
        shards,
        mesh=mesh,
        in_specs=(P("vec", "orb", None), P(), P()),
        out_specs=(P(("orb", "vec"), None, None), P(("orb", "vec"), None)),
        check_vma=False,
    )
```

```python
import jax
import jax.numpy as jnp
from jax import lax
from jax.experimental import pallas as pl
from jax.experimental.pallas import tpu as pltpu
from jax.sharding import PartitionSpec as P

MESH = pl.DeviceIdType.MESH
F32 = jnp.float32
BF16 = jnp.bfloat16
NT = (((1,), (1,)), ((), ()))
TN = (((0,), (0,)), ((), ()))


def kernel(
    chol, coeff_h, density, out, fock,
    chol_v, coeff_t, coeff_blk, density_v, half32, rows_out, rows_in, rows32,
    turn_out, turn_in, part32, pair_in, part_out, part_in, sum32, block_out, gathered, ints,
    chol_sem, coeff_sem, density_sem, pair_send, pair_recv, rows_send, rows_recv, part_send, part_recv,
    turn_send, turn_recv, block_send, block_recv,
):
    vec, orb = lax.axis_index("vec"), lax.axis_index("orb")
    x, zh, y = vec // 16, (vec // 4) % 4, vec % 4
    zl, core = orb // 2, orb % 2

    def plane(k):
        return (((x + k // 4) % 4) * 16 + zh * 4 + (y + k % 4) % 4, orb)

    def column(k):
        to = (zh * 4 + zl + k) % 16
        return (x * 16 + (to // 4) * 4 + y, (to % 4) * 2 + core)

    def column_to(z):
        return (z - zh * 4 - zl + 16) % 16

    def plane_to(n):
        return ((n // 4 - x + 4) % 4) * 4 + (n % 4 - y + 4) % 4

    sibling = (vec, zl * 2 + 1 - core)

    def chips(n):
        vec_to, _ = plane(n // 2)
        return (vec_to, zl * 2 + (core + n) % 2)

    def remote(src, dst, send, recv, device):
        return pltpu.make_async_remote_copy(
            src_ref=src, dst_ref=dst, send_sem=send, recv_sem=recv, device_id=device, device_id_type=MESH
        )

    def fetch(n):
        piece = (slice(None), slice(None), pl.ds(n * 512, 512))
        return pltpu.make_async_copy(chol.at[piece], chol_v.at[piece], chol_sem.at[n])

    coeff_copy = pltpu.make_async_copy(coeff_h, coeff_t, coeff_sem)
    coeff_copy.start()
    for n in range(4):
        fetch(n).start()
    density_copy = pltpu.make_async_copy(density, density_v, density_sem)

    barrier = pltpu.get_barrier_semaphore()

    pl.semaphore_signal(barrier, inc=1, device_id=sibling, device_id_type=MESH)

    @pl.loop(0, 16)
    def _(n):
        k = column_to(n)
        p = plane_to(n)

        @pl.when(k != 0)
        def _():
            pl.semaphore_signal(barrier, inc=1, device_id=column(k), device_id_type=MESH)

        @pl.when(p != 0)
        def _():
            pl.semaphore_signal(barrier, inc=1, device_id=chips(2 * p + 1 - core), device_id_type=MESH)
            pl.semaphore_signal(barrier, inc=1, device_id=chips(2 * p + core), device_id_type=MESH)

    coeff_copy.wait()
    for n in range(2):
        lanes = pl.ds(pl.multiple_of(orb * 256 + n * 128, 128), 128)
        coeff_blk[n * 24 : n * 24 + 24, :] = coeff_t[:, lanes].astype(F32)
    coeff_rows = jnp.concatenate(
        [
            jnp.concatenate([coeff_blk[pl.ds(n * 24 + k, 8, stride=3), :] for k in range(3)], axis=0)
            for n in range(2)
        ],
        axis=1,
    ).astype(BF16)

    turned = None
    half32[...] = jnp.zeros_like(half32)
    for n in range(4):
        fetch(n).wait()
        term = lax.dot_general(
            coeff_t[:, n * 512 : n * 512 + 512],
            chol_v[:, :, n * 512 : n * 512 + 512].reshape(1024, 512),
            NT,
            preferred_element_type=F32,
        )
        turned = turned + term if n else term
    density_copy.start()
    turned = turned.astype(BF16)
    stacked = jnp.concatenate([turned[:, q * 256 : q * 256 + 256] for q in range(4)], axis=0)
    part = lax.dot_general(coeff_rows, stacked, NT, preferred_element_type=F32)
    part = jnp.concatenate([part, jnp.zeros((24, 32), F32)], axis=1)
    lane8 = lax.broadcasted_iota(jnp.int32, (8, 128), 1)
    for q in range(4):
        packed = jnp.zeros((8, 128), F32)
        for k in range(3):
            piece = part[k * 8 : k * 8 + 8]
            shift = (24 * (k - q)) % 128
            piece = pltpu.roll(piece, shift, 1) if shift else piece
            packed = jnp.where((lane8 >= 24 * k) & (lane8 < 24 * k + 24), piece, packed)
        part32[0, q * 4 : q * 4 + 4, :] = packed[0:4]
        part32[1, q * 4 : q * 4 + 4, :] = packed[4:8]

    pl.semaphore_wait(barrier, 46)

    pair_copy = remote(part32.at[1 - core], pair_in, pair_send, pair_recv, sibling)
    pair_copy.start()

    half32[:, 0:24] = turned.astype(F32).T

    lane = lax.broadcasted_iota(jnp.int32, (16, 128), 1)
    for zz in range(4):
        tiles = [None] * 3
        for n in range(16):
            at, shift = divmod(24 * n, 128)
            group = half32[pl.ds(zz * 16 + n, 16, stride=64), :]
            group = pltpu.roll(group, shift, 1) if shift else group
            if shift > 104:
                tiles[at + 1] = jnp.where(lane < shift, group, 0.0)
                group = jnp.where(lane >= shift, group, 0.0)
            tiles[at] = group if tiles[at] is None else tiles[at] + group
        for n in range(3):
            rows_out[zz, :, n * 128 : n * 128 + 128] = tiles[n].astype(BF16)

    def rows_copy(k):
        to = (zh + k) % 4
        device = (x * 16 + to * 4 + y, orb)
        return remote(rows_out.at[to], rows_in.at[k], rows_send.at[k], rows_recv.at[k], device)

    @pl.loop(1, 4)
    def _(k):
        rows_copy(k).start()

    pair_copy.wait_recv()
    mine = (part32[core] + pair_in[...]).astype(BF16)
    part_out[...] = mine
    part_in[0] = mine

    def part_copy(k):
        return remote(part_out, part_in.at[k], part_send.at[k], part_recv.at[k], column(k))

    @pl.loop(0, 16)
    def _(n):
        k = column_to(n)

        @pl.when(k != 0)
        def _():
            part_copy(k).start()

    rows_in[0] = rows_out[zh]

    @pl.loop(1, 4)
    def _(k):
        rows_copy(k).wait_recv()

    for k in range(4):
        for n in range(3):
            rows32[n * 64 + k * 16 : n * 64 + k * 16 + 16, :] = rows_in[k, :, n * 128 : n * 128 + 128].astype(F32)
    for xx in range(4):
        t = [rows32[pl.ds(n * 64 + xx, 16, stride=4), :] for n in range(3)]
        owners = (
            t[0],
            jnp.where(lane < 32, pltpu.roll(t[0], 32, 1), pltpu.roll(t[1], 32, 1)),
            jnp.where(lane < 64, pltpu.roll(t[1], 64, 1), pltpu.roll(t[2], 64, 1)),
            pltpu.roll(t[2], 96, 1),
        )
        for yy in range(4):
            turn_out[xx * 4 + yy] = owners[yy].astype(BF16)

    def turn_copy(k):
        to = ((x + k // 4) % 4) * 4 + (y + k % 4) % 4
        return remote(turn_out.at[to], turn_in.at[k], turn_send.at[k], turn_recv.at[k], plane(k))

    @pl.loop(0, 16)
    def _(n):
        k = plane_to(n)

        @pl.when(k != 0)
        def _():
            turn_copy(k).start()

    turn_in[0] = turn_out[x * 4 + y]

    @pl.loop(1, 16)
    def _(k):
        part_copy(k).wait_recv()

    for h in range(4):
        total = part_in[(4 * h + zl) % 16].astype(F32)
        for n in range(1, 4):
            total = total + part_in[(4 * h + zl - n + 16) % 16].astype(F32)
        sum32[h * 16 : h * 16 + 16, :] = total
    piece = [sum32[pl.ds(j, 16, stride=4), :] for j in range(4)]
    one, two, three = pltpu.roll(piece[1], 72, 1), pltpu.roll(piece[2], 16, 1), pltpu.roll(piece[3], 88, 1)
    left = (piece[0] + jnp.where(lane >= 72, one, 0.0)).astype(BF16)
    middle = (jnp.where(lane < 16, one, 0.0) + two + jnp.where(lane >= 88, three, 0.0)).astype(BF16)
    right = jnp.where(lane < 32, three, 0.0).astype(BF16)
    for n, tile in enumerate((left, middle, right)):
        block_out[:, n * 128 : n * 128 + 128] = tile
        gathered[core, 0, :, n * 128 : n * 128 + 128] = tile

    def block_copy(n, source):
        there = gathered.at[source, n // 2]
        return remote(block_out, there, block_send.at[n], block_recv.at[source, n // 2], chips(n))

    block_copy(1, core).start()

    @pl.loop(0, 16)
    def _(n):
        k = plane_to(n)

        @pl.when(k != 0)
        def _():
            block_copy(2 * k + 1 - core, core).start()
            block_copy(2 * k + core, core).start()

    @pl.loop(1, 16)
    def _(k):
        block_copy(2 * k, core).wait_recv()
        block_copy(2 * k, 1 - core).wait_recv()

    block_copy(1, 1 - core).wait_recv()

    @pl.loop(1, 16)
    def _(k):
        turn_copy(k).wait_recv()

    own = turn_in[...].reshape(256, 128)[:, 0:96]
    first = lax.dot_general(own, gathered[0].reshape(256, 384), TN, preferred_element_type=F32)
    second = lax.dot_general(own, gathered[1].reshape(256, 384), TN, preferred_element_type=F32)
    lane = lax.broadcasted_iota(jnp.int32, (96, 128), 1)
    a, b, c = (pltpu.roll(second[:, n * 128 : n * 128 + 128], 32, 1) for n in range(3))
    tiles = (
        first[:, 0:128],
        first[:, 128:256],
        first[:, 256:384] + jnp.where(lane >= 32, a, 0.0),
        jnp.where(lane < 32, a, b),
        jnp.where(lane < 32, b, c),
    )
    for n, tile in enumerate(tiles):
        width = min(128, 576 - n * 128)
        tile = tile[:, 0:width]
        out[:, :, n * 128 : n * 128 + width] = tile.reshape(4, 24, width)
        high = tile.astype(BF16)
        ints[0:96, n * 128 : n * 128 + width] = high
        ints[96:192, n * 128 : n * 128 + width] = (tile - high.astype(F32)).astype(BF16)

    density_copy.wait()
    pairs = lax.dot_general(ints[...], density_v[...], NT, preferred_element_type=F32)
    pairs = pairs[0:96] + pairs[96:192]
    row = lax.broadcasted_iota(jnp.int32, (96, 576), 0) % 24
    col = lax.broadcasted_iota(jnp.int32, (96, 576), 1) % 24
    kept = jnp.where(row == col, pairs, 0.0).reshape(4, 24, 576).sum(axis=1)
    pick = lax.broadcasted_iota(jnp.int32, (576, 24), 0) // 24 == lax.broadcasted_iota(jnp.int32, (576, 24), 1)
    fock[...] = jnp.dot(kept, pick.astype(F32), precision=lax.Precision.HIGHEST, preferred_element_type=F32)

    pair_copy.wait_send()
    block_copy(1, core).wait_send()

    @pl.loop(1, 16)
    def _(k):
        turn_copy(k).wait_send()
        part_copy(k).wait_send()
        block_copy(2 * k, core).wait_send()
        block_copy(2 * k + 1, core).wait_send()

    @pl.loop(1, 4)
    def _(k):
        rows_copy(k).wait_send()


def shards(cholesky, active_coeff, pair_density):
    vmem = pl.BlockSpec(memory_space=pltpu.VMEM)
    hbm = pl.BlockSpec(memory_space=pltpu.HBM)
    dma = pltpu.SemaphoreType.DMA
    return pl.pallas_call(
        kernel,
        name="half_active_fock",
        out_shape=(jax.ShapeDtypeStruct((4, 24, 576), F32), jax.ShapeDtypeStruct((4, 24), F32)),
        in_specs=[hbm, hbm, hbm],
        out_specs=(vmem, vmem),
        scratch_shapes=[
            pltpu.VMEM((4, 256, 2048), BF16),
            pltpu.VMEM((24, 2048), BF16),
            pltpu.VMEM((48, 128), F32),
            pltpu.VMEM((576, 576), BF16),
            pltpu.VMEM((1024, 128), F32),
            pltpu.VMEM((4, 16, 384), BF16),
            pltpu.VMEM((4, 16, 384), BF16),
            pltpu.VMEM((192, 128), F32),
            pltpu.VMEM((16, 16, 128), BF16),
            pltpu.VMEM((16, 16, 128), BF16),
            pltpu.VMEM((2, 16, 128), F32),
            pltpu.VMEM((16, 128), F32),
            pltpu.VMEM((16, 128), BF16),
            pltpu.VMEM((16, 16, 128), BF16),
            pltpu.VMEM((64, 128), F32),
            pltpu.VMEM((16, 384), BF16),
            pltpu.VMEM((2, 16, 16, 384), BF16),
            pltpu.VMEM((192, 576), BF16),
            dma((4,)), dma, dma, dma, dma, dma((4,)), dma((4,)), dma((16,)), dma((16,)),
            dma((16,)), dma((16,)), dma((32,)), dma((2, 16)),
        ],
        compiler_params=pltpu.CompilerParams(
            collective_id=0, has_side_effects=True, vmem_limit_bytes=16 * 2**20
        ),
    )(
        *(
            pltpu.with_memory_space_constraint(array, pltpu.HBM)
            for array in (cholesky, active_coeff.T, pair_density.reshape(576, 576))
        )
    )


def solution(mesh):
    return jax.shard_map(
        shards,
        mesh=mesh,
        in_specs=(P("vec", "orb", None), P(), P()),
        out_specs=(P(("orb", "vec"), None, None), P(("orb", "vec"), None)),
        check_vma=False,
    )
```

```python
import jax
import jax.numpy as jnp
from jax import lax
from jax.experimental import pallas as pl
from jax.experimental.pallas import tpu as pltpu
from jax.sharding import PartitionSpec as P

MESH = pl.DeviceIdType.MESH
F32 = jnp.float32
BF16 = jnp.bfloat16
NT = (((1,), (1,)), ((), ()))
TN = (((0,), (0,)), ((), ()))

CUTS = (0, 512, 1024, 1536, 1792, 2048)


def kernel(
    chol, coeff_h, out,
    chol_v, coeff_t, coeff_blk, half32, rows_out, rows_in, rows32,
    turn_out, turn_in, part32, pair_in, part_out, part_in, sum32, block_out, gathered,
    chol_sem, coeff_sem, pair_send, pair_recv, rows_send, rows_recv, part_send, part_recv,
    turn_send, turn_recv, block_send, block_recv,
):
    vec, orb = lax.axis_index("vec"), lax.axis_index("orb")
    x, zh, y = vec // 16, (vec // 4) % 4, vec % 4
    zl, core = orb // 2, orb % 2

    def plane(k):
        return (((x + k // 4) % 4) * 16 + zh * 4 + (y + k % 4) % 4, orb)

    def column(k):
        to = (zh * 4 + zl + k) % 16
        return (x * 16 + (to // 4) * 4 + y, (to % 4) * 2 + core)

    def column_to(z):
        return (z - zh * 4 - zl + 16) % 16

    def plane_to(n):
        return ((n // 4 - x + 4) % 4) * 4 + (n % 4 - y + 4) % 4

    sibling = (vec, zl * 2 + 1 - core)

    def chips(n):
        vec_to, _ = plane(n // 2)
        return (vec_to, zl * 2 + (core + n) % 2)

    def quad(n):
        return (vec, ((zl // 2) * 2 + (zl + n // 2) % 2) * 2 + (core + n) % 2)

    def remote(src, dst, send, recv, device):
        return pltpu.make_async_remote_copy(
            src_ref=src, dst_ref=dst, send_sem=send, recv_sem=recv, device_id=device, device_id_type=MESH
        )

    def fetch(n):
        piece = (slice(None), slice(None), pl.ds(CUTS[n], CUTS[n + 1] - CUTS[n]))
        return pltpu.make_async_copy(chol.at[piece], chol_v.at[piece], chol_sem.at[n])

    coeff_copy = pltpu.make_async_copy(coeff_h, coeff_t, coeff_sem)
    coeff_copy.start()
    for n in range(len(CUTS) - 1):
        fetch(n).start()

    barrier = pltpu.get_barrier_semaphore()

    @pl.loop(0, 16)
    def _(n):
        k = column_to(n)

        @pl.when(k != 0)
        def _():
            pl.semaphore_signal(barrier, inc=1, device_id=column(k), device_id_type=MESH)

    pl.semaphore_signal(barrier, inc=1, device_id=sibling, device_id_type=MESH)
    pl.semaphore_signal(barrier, inc=1, device_id=quad(3), device_id_type=MESH)

    @pl.loop(0, 16)
    def _(n):
        k = plane_to(n)

        @pl.when(k != 0)
        def _():
            pl.semaphore_signal(barrier, inc=1, device_id=chips(2 * k + 1 - core), device_id_type=MESH)
            pl.semaphore_signal(barrier, inc=1, device_id=chips(2 * k + core), device_id_type=MESH)

    coeff_copy.wait()
    for n in range(2):
        lanes = pl.ds(pl.multiple_of(orb * 256 + n * 128, 128), 128)
        coeff_blk[n * 24 : n * 24 + 24, :] = coeff_t[:, lanes].astype(F32)
    coeff_rows = jnp.concatenate(
        [
            jnp.concatenate([coeff_blk[pl.ds(n * 24 + k, 8, stride=3), :] for k in range(3)], axis=0)
            for n in range(2)
        ],
        axis=1,
    ).astype(BF16)

    turned = None
    half32[...] = jnp.zeros_like(half32)
    for n in range(len(CUTS) - 1):
        fetch(n).wait()
        columns = slice(CUTS[n], CUTS[n + 1])
        term = lax.dot_general(
            coeff_t[:, columns],
            chol_v[:, :, columns].reshape(1024, -1),
            NT,
            preferred_element_type=F32,
        )
        turned = turned + term if n else term
    turned = turned.astype(BF16)
    stacked = jnp.concatenate([turned[:, q * 256 : q * 256 + 256] for q in range(4)], axis=0)
    part = lax.dot_general(coeff_rows, stacked, NT, preferred_element_type=F32)
    part = jnp.concatenate([part, jnp.zeros((24, 32), F32)], axis=1)
    lane8 = lax.broadcasted_iota(jnp.int32, (8, 128), 1)
    for q in range(4):
        packed = jnp.zeros((8, 128), F32)
        for k in range(3):
            piece = part[k * 8 : k * 8 + 8]
            shift = (24 * (k - q)) % 128
            piece = pltpu.roll(piece, shift, 1) if shift else piece
            packed = jnp.where((lane8 >= 24 * k) & (lane8 < 24 * k + 24), piece, packed)
        at = (q % 2) * 4
        part32[0, q // 2, at : at + 4, :] = packed[0:4]
        part32[1, q // 2, at : at + 4, :] = packed[4:8]

    pl.semaphore_wait(barrier, 47)

    def pair_copy(n):
        share = part32.at[(core + n) % 2, (zl + n // 2) % 2]
        return remote(share, pair_in.at[n], pair_send.at[n], pair_recv.at[n], quad(n))

    for n in (3, 2, 1):
        pair_copy(n).start()

    half32[:, 0:24] = turned.astype(F32).T

    lane = lax.broadcasted_iota(jnp.int32, (16, 128), 1)
    for zz in range(4):
        tiles = [None] * 3
        for n in range(16):
            at, shift = divmod(24 * n, 128)
            group = half32[pl.ds(zz * 16 + n, 16, stride=64), :]
            group = pltpu.roll(group, shift, 1) if shift else group
            if shift > 104:
                tiles[at + 1] = jnp.where(lane < shift, group, 0.0)
                group = jnp.where(lane >= shift, group, 0.0)
            tiles[at] = group if tiles[at] is None else tiles[at] + group
        for n in range(3):
            rows_out[zz, :, n * 128 : n * 128 + 128] = tiles[n].astype(BF16)

    def rows_copy(k):
        to = (zh + k) % 4
        device = (x * 16 + to * 4 + y, orb)
        return remote(rows_out.at[to], rows_in.at[k], rows_send.at[k], rows_recv.at[k], device)

    @pl.loop(1, 4)
    def _(k):
        rows_copy(k).start()

    for n in (1, 2, 3):
        pair_copy(n).wait_recv()
    mine = (part32[core, zl % 2] + pair_in[1] + pair_in[2] + pair_in[3]).astype(BF16)
    part_out[...] = mine
    part_in[0] = mine

    def part_copy(k):
        return remote(part_out, part_in.at[k], part_send.at[k], part_recv.at[k], column(k))

    @pl.loop(0, 16)
    def _(n):
        k = column_to(n)

        @pl.when(k != 0)
        def _():
            part_copy(k).start()

    rows_in[0] = rows_out[zh]

    @pl.loop(1, 4)
    def _(k):
        rows_copy(k).wait_recv()

    for k in range(4):
        for n in range(3):
            rows32[n * 64 + k * 16 : n * 64 + k * 16 + 16, :] = rows_in[k, :, n * 128 : n * 128 + 128].astype(F32)
    for xx in range(4):
        t = [rows32[pl.ds(n * 64 + xx, 16, stride=4), :] for n in range(3)]
        owners = (
            t[0],
            jnp.where(lane < 32, pltpu.roll(t[0], 32, 1), pltpu.roll(t[1], 32, 1)),
            jnp.where(lane < 64, pltpu.roll(t[1], 64, 1), pltpu.roll(t[2], 64, 1)),
            pltpu.roll(t[2], 96, 1),
        )
        for yy in range(4):
            turn_out[xx * 4 + yy] = owners[yy].astype(BF16)

    def turn_copy(k):
        to = ((x + k // 4) % 4) * 4 + (y + k % 4) % 4
        return remote(turn_out.at[to], turn_in.at[k], turn_send.at[k], turn_recv.at[k], plane(k))

    turn_in[0] = turn_out[x * 4 + y]

    @pl.loop(1, 16)
    def _(k):
        part_copy(k).wait_recv()

    for h in range(4):
        for p in range(2):
            total = part_in[(4 * h + zl - p + 16) % 16].astype(F32) + part_in[(4 * h + zl - p + 14) % 16].astype(F32)
            sum32[h * 16 + p * 8 : h * 16 + p * 8 + 8, :] = total
    piece = [sum32[pl.ds(j, 16, stride=4), :] for j in range(4)]
    one, two, three = pltpu.roll(piece[1], 72, 1), pltpu.roll(piece[2], 16, 1), pltpu.roll(piece[3], 88, 1)
    left = (piece[0] + jnp.where(lane >= 72, one, 0.0)).astype(BF16)
    middle = (jnp.where(lane < 16, one, 0.0) + two + jnp.where(lane >= 88, three, 0.0)).astype(BF16)
    right = jnp.where(lane < 32, three, 0.0).astype(BF16)
    for n, tile in enumerate((left, middle, right)):
        block_out[:, n * 128 : n * 128 + 128] = tile
        gathered[core, 0, :, n * 128 : n * 128 + 128] = tile

    def block_copy(n, source):
        there = gathered.at[source, n // 2]
        return remote(block_out, there, block_send.at[n], block_recv.at[source, n // 2], chips(n))

    block_copy(1, core).start()

    @pl.loop(0, 16)
    def _(n):
        k = plane_to(n)

        @pl.when(k != 0)
        def _():
            block_copy(2 * k + 1 - core, core).start()
            block_copy(2 * k + core, core).start()
            turn_copy(k).start()

    @pl.loop(1, 16)
    def _(k):
        block_copy(2 * k, core).wait_recv()
        block_copy(2 * k, 1 - core).wait_recv()

    block_copy(1, 1 - core).wait_recv()

    @pl.loop(1, 16)
    def _(k):
        turn_copy(k).wait_recv()

    own = turn_in[...].reshape(256, 128)[:, 0:96]
    first = lax.dot_general(own, gathered[0].reshape(256, 384), TN, preferred_element_type=F32)
    second = lax.dot_general(own, gathered[1].reshape(256, 384), TN, preferred_element_type=F32)
    lane = lax.broadcasted_iota(jnp.int32, (96, 128), 1)
    a, b, c = (pltpu.roll(second[:, n * 128 : n * 128 + 128], 32, 1) for n in range(3))
    tiles = (
        first[:, 0:128],
        first[:, 128:256],
        first[:, 256:384] + jnp.where(lane >= 32, a, 0.0),
        jnp.where(lane < 32, a, b),
        jnp.where(lane < 32, b, c),
    )
    for n, tile in enumerate(tiles):
        width = min(128, 576 - n * 128)
        tile = tile[:, 0:width]
        out[:, :, n * 128 : n * 128 + width] = tile.reshape(4, 24, width)

    for n in (1, 2, 3):
        pair_copy(n).wait_send()
    block_copy(1, core).wait_send()

    @pl.loop(1, 16)
    def _(k):
        turn_copy(k).wait_send()
        part_copy(k).wait_send()
        block_copy(2 * k, core).wait_send()
        block_copy(2 * k + 1, core).wait_send()

    @pl.loop(1, 4)
    def _(k):
        rows_copy(k).wait_send()


def fock_kernel(ints, density, out, fock, split, out_sem):
    copy = pltpu.make_async_copy(ints, out, out_sem)
    copy.start()
    tile = ints[...].reshape(96, 576)
    high = tile.astype(BF16)
    split[0:96, :] = high
    split[96:192, :] = (tile - high.astype(F32)).astype(BF16)

    pairs = lax.dot_general(split[...], density[...], NT, preferred_element_type=F32)
    pairs = pairs[0:96] + pairs[96:192]
    row = lax.broadcasted_iota(jnp.int32, (96, 576), 0) % 24
    col = lax.broadcasted_iota(jnp.int32, (96, 576), 1) % 24
    kept = jnp.where(row == col, pairs, 0.0).reshape(4, 24, 576).sum(axis=1)
    pick = lax.broadcasted_iota(jnp.int32, (576, 24), 0) // 24 == lax.broadcasted_iota(jnp.int32, (576, 24), 1)
    fock[...] = jnp.dot(kept, pick.astype(F32), precision=lax.Precision.HIGHEST, preferred_element_type=F32)
    copy.wait()


def shards(cholesky, active_coeff, pair_density):
    vmem = pl.BlockSpec(memory_space=pltpu.VMEM)
    hbm = pl.BlockSpec(memory_space=pltpu.HBM)
    dma = pltpu.SemaphoreType.DMA
    ints = pl.pallas_call(
        kernel,
        name="half_active_fock",
        out_shape=jax.ShapeDtypeStruct((4, 24, 576), F32),
        in_specs=[hbm, hbm],
        out_specs=vmem,
        scratch_shapes=[
            pltpu.VMEM((4, 256, 2048), BF16),
            pltpu.VMEM((24, 2048), BF16),
            pltpu.VMEM((48, 128), F32),
            pltpu.VMEM((1024, 128), F32),
            pltpu.VMEM((4, 16, 384), BF16),
            pltpu.VMEM((4, 16, 384), BF16),
            pltpu.VMEM((192, 128), F32),
            pltpu.VMEM((16, 16, 128), BF16),
            pltpu.VMEM((16, 16, 128), BF16),
            pltpu.VMEM((2, 2, 8, 128), F32),
            pltpu.VMEM((4, 8, 128), F32),
            pltpu.VMEM((8, 128), BF16),
            pltpu.VMEM((16, 8, 128), BF16),
            pltpu.VMEM((64, 128), F32),
            pltpu.VMEM((16, 384), BF16),
            pltpu.VMEM((2, 16, 16, 384), BF16),
            dma((len(CUTS) - 1,)), dma, dma((4,)), dma((4,)), dma((4,)), dma((4,)), dma((16,)), dma((16,)),
            dma((16,)), dma((16,)), dma((32,)), dma((2, 16)),
        ],
        compiler_params=pltpu.CompilerParams(
            collective_id=0, has_side_effects=True, vmem_limit_bytes=16 * 2**20
        ),
    )(*(pltpu.with_memory_space_constraint(array, pltpu.HBM) for array in (cholesky, active_coeff.T)))
    return pl.pallas_call(
        fock_kernel,
        name="fock",
        out_shape=(jax.ShapeDtypeStruct((4, 24, 576), F32), jax.ShapeDtypeStruct((4, 24), F32)),
        in_specs=[vmem, vmem],
        out_specs=(hbm, vmem),
        scratch_shapes=[pltpu.VMEM((192, 576), BF16), dma],
        compiler_params=pltpu.CompilerParams(vmem_limit_bytes=16 * 2**20),
    )(ints, pair_density.reshape(576, 576))


def solution(mesh):
    return jax.shard_map(
        shards,
        mesh=mesh,
        in_specs=(P("vec", "orb", None), P(), P()),
        out_specs=(P(("orb", "vec"), None, None), P(("orb", "vec"), None)),
        check_vma=False,
    )
```

```python
import jax
import jax.numpy as jnp
from jax import lax
from jax.experimental import pallas as pl
from jax.experimental.pallas import tpu as pltpu
from jax.sharding import PartitionSpec as P

MESH = pl.DeviceIdType.MESH
F32 = jnp.float32
BF16 = jnp.bfloat16
NT = (((1,), (1,)), ((), ()))
TN = (((0,), (0,)), ((), ()))

CUTS = (0, 512, 1024, 1536, 1792, 2048)


def kernel(
    chol, coeff_h, out,
    chol_v, coeff_t, coeff_blk, half32, rows_out, rows_in, rows32,
    turn_out, turn_in, part32, pair_in, part_out, part_in, sum32, block_out, gathered,
    chol_sem, coeff_sem, pair_send, pair_recv, rows_send, rows_recv, part_send, part_recv,
    turn_send, turn_recv, block_send, block_recv, share_send, share_recv,
):
    vec, orb = lax.axis_index("vec"), lax.axis_index("orb")
    x, zh, y = vec // 16, (vec // 4) % 4, vec % 4
    zl, core = orb // 2, orb % 2

    def plane(k):
        return (((x + k // 4) % 4) * 16 + zh * 4 + (y + k % 4) % 4, orb)

    def column(k):
        to = (zh * 4 + zl + k) % 16
        return (x * 16 + (to // 4) * 4 + y, (to % 4) * 2 + core)

    def column_to(z):
        return (z - zh * 4 - zl + 16) % 16

    def plane_to(n):
        return ((n // 4 - x + 4) % 4) * 4 + (n % 4 - y + 4) % 4

    sibling = (vec, zl * 2 + 1 - core)

    def chips(n):
        vec_to, _ = plane(n // 2)
        return (vec_to, zl * 2 + (core + n) % 2)

    def quad(n):
        return (vec, ((zl // 2) * 2 + (zl + n // 2) % 2) * 2 + (core + n) % 2)

    def remote(src, dst, send, recv, device):
        return pltpu.make_async_remote_copy(
            src_ref=src, dst_ref=dst, send_sem=send, recv_sem=recv, device_id=device, device_id_type=MESH
        )

    def fetch(n):
        piece = (slice(None), slice(None), pl.ds(CUTS[n], CUTS[n + 1] - CUTS[n]))
        return pltpu.make_async_copy(chol.at[piece], chol_v.at[piece], chol_sem.at[n])

    coeff_copy = pltpu.make_async_copy(coeff_h, coeff_t, coeff_sem)
    coeff_copy.start()
    for n in range(len(CUTS) - 1):
        fetch(n).start()

    barrier = pltpu.get_barrier_semaphore()

    @pl.loop(0, 16)
    def _(n):
        k = column_to(n)

        @pl.when(k != 0)
        def _():
            pl.semaphore_signal(barrier, inc=1, device_id=column(k), device_id_type=MESH)

    pl.semaphore_signal(barrier, inc=1, device_id=sibling, device_id_type=MESH)
    pl.semaphore_signal(barrier, inc=1, device_id=quad(3), device_id_type=MESH)

    @pl.loop(0, 16)
    def _(n):
        k = plane_to(n)

        @pl.when(k != 0)
        def _():
            pl.semaphore_signal(barrier, inc=1, device_id=chips(2 * k + 1 - core), device_id_type=MESH)
            pl.semaphore_signal(barrier, inc=1, device_id=chips(2 * k + core), device_id_type=MESH)

    coeff_copy.wait()
    for n in range(2):
        lanes = pl.ds(pl.multiple_of(orb * 256 + n * 128, 128), 128)
        coeff_blk[n * 24 : n * 24 + 24, :] = coeff_t[:, lanes].astype(F32)
    coeff_rows = jnp.concatenate(
        [
            jnp.concatenate([coeff_blk[pl.ds(n * 24 + k, 8, stride=3), :] for k in range(3)], axis=0)
            for n in range(2)
        ],
        axis=1,
    ).astype(BF16)

    turned = None
    half32[...] = jnp.zeros_like(half32)
    for n in range(len(CUTS) - 1):
        fetch(n).wait()
        columns = slice(CUTS[n], CUTS[n + 1])
        term = lax.dot_general(
            coeff_t[:, columns],
            chol_v[:, :, columns].reshape(1024, -1),
            NT,
            preferred_element_type=F32,
        )
        turned = turned + term if n else term
    turned = turned.astype(BF16)
    stacked = jnp.concatenate([turned[:, q * 256 : q * 256 + 256] for q in range(4)], axis=0)
    part = lax.dot_general(coeff_rows, stacked, NT, preferred_element_type=F32)
    part = jnp.concatenate([part, jnp.zeros((24, 32), F32)], axis=1)
    lane8 = lax.broadcasted_iota(jnp.int32, (8, 128), 1)
    for q in range(4):
        packed = jnp.zeros((8, 128), F32)
        for k in range(3):
            piece = part[k * 8 : k * 8 + 8]
            shift = (24 * (k - q)) % 128
            piece = pltpu.roll(piece, shift, 1) if shift else piece
            packed = jnp.where((lane8 >= 24 * k) & (lane8 < 24 * k + 24), piece, packed)
        at = (q % 2) * 4
        part32[0, q // 2, at : at + 4, :] = packed[0:4]
        part32[1, q // 2, at : at + 4, :] = packed[4:8]

    pl.semaphore_wait(barrier, 47)

    def pair_copy(n):
        share = part32.at[(core + n) % 2, (zl + n // 2) % 2]
        return remote(share, pair_in.at[n], pair_send.at[n], pair_recv.at[n], quad(n))

    for n in (3, 2, 1):
        pair_copy(n).start()

    half32[:, 0:24] = turned.astype(F32).T

    lane = lax.broadcasted_iota(jnp.int32, (16, 128), 1)
    for zz in range(4):
        tiles = [None] * 3
        for n in range(16):
            at, shift = divmod(24 * n, 128)
            group = half32[pl.ds(zz * 16 + n, 16, stride=64), :]
            group = pltpu.roll(group, shift, 1) if shift else group
            if shift > 104:
                tiles[at + 1] = jnp.where(lane < shift, group, 0.0)
                group = jnp.where(lane >= shift, group, 0.0)
            tiles[at] = group if tiles[at] is None else tiles[at] + group
        for n in range(3):
            rows_out[zz, :, n * 128 : n * 128 + 128] = tiles[n].astype(BF16)

    def rows_copy(k):
        to = (zh + k) % 4
        device = (x * 16 + to * 4 + y, orb)
        return remote(rows_out.at[to], rows_in.at[k], rows_send.at[k], rows_recv.at[k], device)

    @pl.loop(1, 4)
    def _(k):
        rows_copy(k).start()

    for n in (1, 2, 3):
        pair_copy(n).wait_recv()
    mine = (part32[core, zl % 2] + pair_in[1] + pair_in[2] + pair_in[3]).astype(BF16)
    part_out[...] = mine
    part_in[0] = mine

    def part_copy(k):
        return remote(part_out, part_in.at[k], part_send.at[k], part_recv.at[k], column(k))

    @pl.loop(0, 16)
    def _(n):
        k = column_to(n)

        @pl.when(k != 0)
        def _():
            part_copy(k).start()

    rows_in[0] = rows_out[zh]

    @pl.loop(1, 4)
    def _(k):
        rows_copy(k).wait_recv()

    for k in range(4):
        for n in range(3):
            rows32[n * 64 + k * 16 : n * 64 + k * 16 + 16, :] = rows_in[k, :, n * 128 : n * 128 + 128].astype(F32)
    for xx in range(4):
        t = [rows32[pl.ds(n * 64 + xx, 16, stride=4), :] for n in range(3)]
        owners = (
            t[0],
            jnp.where(lane < 32, pltpu.roll(t[0], 32, 1), pltpu.roll(t[1], 32, 1)),
            jnp.where(lane < 64, pltpu.roll(t[1], 64, 1), pltpu.roll(t[2], 64, 1)),
            pltpu.roll(t[2], 96, 1),
        )
        for yy in range(4):
            turn_out[xx * 4 + yy] = owners[yy].astype(BF16)

    def turn_copy(k):
        to = ((x + k // 4) % 4) * 4 + (y + k % 4) % 4
        return remote(turn_out.at[to], turn_in.at[k], turn_send.at[k], turn_recv.at[k], plane(k))

    @pl.loop(0, 16)
    def _(n):
        k = plane_to(n)

        @pl.when(k != 0)
        def _():
            turn_copy(k).start()

    turn_in[0] = turn_out[x * 4 + y]

    @pl.loop(1, 16)
    def _(k):
        part_copy(k).wait_recv()

    for h in range(4):
        for p in range(2):
            total = part_in[(4 * h + zl - p + 16) % 16].astype(F32) + part_in[(4 * h + zl - p + 14) % 16].astype(F32)
            sum32[h * 16 + p * 8 : h * 16 + p * 8 + 8, :] = total
    piece = [sum32[pl.ds(j, 16, stride=4), :] for j in range(4)]
    one, two, three = pltpu.roll(piece[1], 72, 1), pltpu.roll(piece[2], 16, 1), pltpu.roll(piece[3], 88, 1)
    left = (piece[0] + jnp.where(lane >= 72, one, 0.0)).astype(BF16)
    middle = (jnp.where(lane < 16, one, 0.0) + two + jnp.where(lane >= 88, three, 0.0)).astype(BF16)
    right = jnp.where(lane < 32, three, 0.0).astype(BF16)
    for n, tile in enumerate((left, middle, right)):
        block_out[:, n * 128 : n * 128 + 128] = tile
        gathered[core, 0, :, n * 128 : n * 128 + 128] = tile

    origin = vec // 16 + vec % 4 == 0

    def block_copy(n, source):
        there = gathered.at[source, n // 2]
        return remote(block_out, there, block_send.at[n], block_recv.at[source, n // 2], chips(n))

    def share_copy(n, source):
        there = gathered.at[source, pl.ds(n * 8, 8)]
        return remote(there, there, share_send.at[n], share_recv.at[n], sibling)

    first_k = plane_to(0)

    @pl.when(first_k != 0)
    def _():
        block_copy(2 * first_k + 1 - core, core).start()
        block_copy(2 * first_k + core, core).start()

    @pl.when(first_k == 0)
    def _():
        block_copy(1, core).start()

    @pl.loop(1, 16)
    def _(n):
        k = plane_to(n)

        @pl.when(k != 0)
        def _():
            block_copy(2 * k, core).start()

    @pl.loop(1, 16)
    def _(k):
        part_copy(k).wait_send()

    @pl.loop(1, 4)
    def _(k):
        rows_copy(k).wait_send()

    for n in (1, 2, 3):
        pair_copy(n).wait_send()

    @pl.when(origin)
    def _():
        @pl.loop(1, 16)
        def _(k):
            block_copy(2 * k, core).wait_recv()
            block_copy(2 * k, 1 - core).wait_recv()

        block_copy(1, 1 - core).wait_recv()

    @pl.when(jnp.logical_not(origin))
    def _():
        for n in range(2):

            @pl.loop(n * 8 + 1 - n, n * 8 + 8)
            def _(k):
                block_copy(2 * k, core).wait_recv()

            share_copy(n, core).start()

        for n in range(2):
            share_copy(n, 1 - core).wait_recv()

    @pl.loop(1, 16)
    def _(k):
        turn_copy(k).wait_recv()

    own = turn_in[...].reshape(256, 128)[:, 0:96]
    first = lax.dot_general(own, gathered[0].reshape(256, 384), TN, preferred_element_type=F32)
    second = lax.dot_general(own, gathered[1].reshape(256, 384), TN, preferred_element_type=F32)
    lane = lax.broadcasted_iota(jnp.int32, (96, 128), 1)
    a, b, c = (pltpu.roll(second[:, n * 128 : n * 128 + 128], 32, 1) for n in range(3))
    tiles = (
        first[:, 0:128],
        first[:, 128:256],
        first[:, 256:384] + jnp.where(lane >= 32, a, 0.0),
        jnp.where(lane < 32, a, b),
        jnp.where(lane < 32, b, c),
    )
    for n, tile in enumerate(tiles):
        width = min(128, 576 - n * 128)
        tile = tile[:, 0:width]
        out[:, :, n * 128 : n * 128 + width] = tile.reshape(4, 24, width)

    @pl.when(origin)
    def _():
        block_copy(1, core).wait_send()

    @pl.when(jnp.logical_not(origin))
    def _():
        block_copy(2 * first_k + 1, core).wait_send()
        for n in range(2):
            share_copy(n, core).wait_send()


    @pl.loop(1, 16)
    def _(k):
        turn_copy(k).wait_send()
        block_copy(2 * k, core).wait_send()


def fock_kernel(ints, density, out, fock, split, out_sem):
    copy = pltpu.make_async_copy(ints, out, out_sem)
    copy.start()
    tile = ints[...].reshape(96, 576)
    high = tile.astype(BF16)
    split[0:96, :] = high
    split[96:192, :] = (tile - high.astype(F32)).astype(BF16)

    pairs = lax.dot_general(split[...], density[...], NT, preferred_element_type=F32)
    pairs = pairs[0:96] + pairs[96:192]
    row = lax.broadcasted_iota(jnp.int32, (96, 576), 0) % 24
    col = lax.broadcasted_iota(jnp.int32, (96, 576), 1) % 24
    kept = jnp.where(row == col, pairs, 0.0).reshape(4, 24, 576).sum(axis=1)
    pick = lax.broadcasted_iota(jnp.int32, (576, 24), 0) // 24 == lax.broadcasted_iota(jnp.int32, (576, 24), 1)
    fock[...] = jnp.dot(kept, pick.astype(F32), precision=lax.Precision.HIGHEST, preferred_element_type=F32)
    copy.wait()


def shards(cholesky, active_coeff, pair_density):
    vmem = pl.BlockSpec(memory_space=pltpu.VMEM)
    hbm = pl.BlockSpec(memory_space=pltpu.HBM)
    dma = pltpu.SemaphoreType.DMA
    ints = pl.pallas_call(
        kernel,
        name="half_active_fock",
        out_shape=jax.ShapeDtypeStruct((4, 24, 576), F32),
        in_specs=[hbm, hbm],
        out_specs=vmem,
        scratch_shapes=[
            pltpu.VMEM((4, 256, 2048), BF16),
            pltpu.VMEM((24, 2048), BF16),
            pltpu.VMEM((48, 128), F32),
            pltpu.VMEM((1024, 128), F32),
            pltpu.VMEM((4, 16, 384), BF16),
            pltpu.VMEM((4, 16, 384), BF16),
            pltpu.VMEM((192, 128), F32),
            pltpu.VMEM((16, 16, 128), BF16),
            pltpu.VMEM((16, 16, 128), BF16),
            pltpu.VMEM((2, 2, 8, 128), F32),
            pltpu.VMEM((4, 8, 128), F32),
            pltpu.VMEM((8, 128), BF16),
            pltpu.VMEM((16, 8, 128), BF16),
            pltpu.VMEM((64, 128), F32),
            pltpu.VMEM((16, 384), BF16),
            pltpu.VMEM((2, 16, 16, 384), BF16),
            dma((len(CUTS) - 1,)), dma, dma((4,)), dma((4,)), dma((4,)), dma((4,)), dma((16,)), dma((16,)),
            dma((16,)), dma((16,)), dma((32,)), dma((2, 16)), dma((2,)), dma((2,)),
        ],
        compiler_params=pltpu.CompilerParams(
            collective_id=0, has_side_effects=True, vmem_limit_bytes=16 * 2**20
        ),
    )(*(pltpu.with_memory_space_constraint(array, pltpu.HBM) for array in (cholesky, active_coeff.T)))
    return pl.pallas_call(
        fock_kernel,
        name="fock",
        out_shape=(jax.ShapeDtypeStruct((4, 24, 576), F32), jax.ShapeDtypeStruct((4, 24), F32)),
        in_specs=[vmem, vmem],
        out_specs=(hbm, vmem),
        scratch_shapes=[pltpu.VMEM((192, 576), BF16), dma],
        compiler_params=pltpu.CompilerParams(vmem_limit_bytes=16 * 2**20),
    )(ints, pair_density.reshape(576, 576))


def solution(mesh):
    return jax.shard_map(
        shards,
        mesh=mesh,
        in_specs=(P("vec", "orb", None), P(), P()),
        out_specs=(P(("orb", "vec"), None, None), P(("orb", "vec"), None)),
        check_vma=False,
    )
```

```python
import jax
import jax.numpy as jnp
from jax import lax
from jax.experimental import pallas as pl
from jax.experimental.pallas import tpu as pltpu
from jax.sharding import PartitionSpec as P

MESH = pl.DeviceIdType.MESH
F32 = jnp.float32
BF16 = jnp.bfloat16
NT = (((1,), (1,)), ((), ()))

CUTS = (0, 512, 1024, 1536, 1792, 2048)


def kernel(
    chol, coeff_h, out,
    chol_v, coeff_t, coeff_blk, half32, rows_out, rows_in, rows32,
    turn_out, turn_in, part32, pair_in, part_out, part_in, sum32, block_out, gathered,
    chol_sem, coeff_sem, pair_send, pair_recv, rows_send, rows_recv, part_send, part_recv,
    turn_send, turn_recv, block_send, block_recv, share_send, share_recv,
):
    vec, orb = lax.axis_index("vec"), lax.axis_index("orb")
    x, zh, y = vec // 16, (vec // 4) % 4, vec % 4
    zl, core = orb // 2, orb % 2

    def plane(k):
        return (((x + k // 4) % 4) * 16 + zh * 4 + (y + k % 4) % 4, orb)

    def column(k):
        to = (zh * 4 + zl + k) % 16
        return (x * 16 + (to // 4) * 4 + y, (to % 4) * 2 + core)

    def column_to(z):
        return (z - zh * 4 - zl + 16) % 16

    def plane_to(n):
        return ((n // 4 - x + 4) % 4) * 4 + (n % 4 - y + 4) % 4

    sibling = (vec, zl * 2 + 1 - core)

    def chips(n):
        vec_to, _ = plane(n // 2)
        return (vec_to, zl * 2 + (core + n) % 2)

    def quad(n):
        return (vec, ((zl // 2) * 2 + (zl + n // 2) % 2) * 2 + (core + n) % 2)

    def remote(src, dst, send, recv, device):
        return pltpu.make_async_remote_copy(
            src_ref=src, dst_ref=dst, send_sem=send, recv_sem=recv, device_id=device, device_id_type=MESH
        )

    def fetch(n):
        piece = (slice(None), slice(None), pl.ds(CUTS[n], CUTS[n + 1] - CUTS[n]))
        return pltpu.make_async_copy(chol.at[piece], chol_v.at[piece], chol_sem.at[n])

    coeff_copy = pltpu.make_async_copy(coeff_h, coeff_t, coeff_sem)
    coeff_copy.start()
    for n in range(len(CUTS) - 1):
        fetch(n).start()

    barrier = pltpu.get_barrier_semaphore()

    @pl.loop(0, 16)
    def _(n):
        k = column_to(n)

        @pl.when(k != 0)
        def _():
            pl.semaphore_signal(barrier, inc=1, device_id=column(k), device_id_type=MESH)

    pl.semaphore_signal(barrier, inc=1, device_id=sibling, device_id_type=MESH)
    pl.semaphore_signal(barrier, inc=1, device_id=quad(3), device_id_type=MESH)

    @pl.loop(0, 16)
    def _(n):
        k = plane_to(n)

        @pl.when(k != 0)
        def _():
            pl.semaphore_signal(barrier, inc=1, device_id=chips(2 * k + 1 - core), device_id_type=MESH)
            pl.semaphore_signal(barrier, inc=1, device_id=chips(2 * k + core), device_id_type=MESH)

    coeff_copy.wait()
    for n in range(2):
        lanes = pl.ds(pl.multiple_of(orb * 256 + n * 128, 128), 128)
        coeff_blk[n * 24 : n * 24 + 24, :] = coeff_t[:, lanes].astype(F32)
    coeff_rows = jnp.concatenate(
        [
            jnp.concatenate([coeff_blk[pl.ds(n * 24 + k, 8, stride=3), :] for k in range(3)], axis=0)
            for n in range(2)
        ],
        axis=1,
    ).astype(BF16)

    turned = None
    half32[...] = jnp.zeros_like(half32)
    for n in range(len(CUTS) - 1):
        fetch(n).wait()
        columns = slice(CUTS[n], CUTS[n + 1])
        term = lax.dot_general(
            coeff_t[:, columns],
            chol_v[:, :, columns].reshape(1024, -1),
            NT,
            preferred_element_type=F32,
        )
        turned = turned + term if n else term
    turned = turned.astype(BF16)
    stacked = jnp.concatenate([turned[:, q * 256 : q * 256 + 256] for q in range(4)], axis=0)
    part = lax.dot_general(coeff_rows, stacked, NT, preferred_element_type=F32)
    part = jnp.concatenate([part, jnp.zeros((24, 32), F32)], axis=1)
    lane8 = lax.broadcasted_iota(jnp.int32, (8, 128), 1)
    for q in range(4):
        packed = jnp.zeros((8, 128), F32)
        for k in range(3):
            piece = part[k * 8 : k * 8 + 8]
            shift = (24 * (k - q)) % 128
            piece = pltpu.roll(piece, shift, 1) if shift else piece
            packed = jnp.where((lane8 >= 24 * k) & (lane8 < 24 * k + 24), piece, packed)
        at = (q % 2) * 4
        part32[0, q // 2, at : at + 4, :] = packed[0:4]
        part32[1, q // 2, at : at + 4, :] = packed[4:8]

    half32[:, 0:24] = turned.astype(F32).T

    lane = lax.broadcasted_iota(jnp.int32, (16, 128), 1)
    for zz in range(4):
        tiles = [None] * 3
        for n in range(16):
            at, shift = divmod(24 * n, 128)
            group = half32[pl.ds(zz * 16 + n, 16, stride=64), :]
            group = pltpu.roll(group, shift, 1) if shift else group
            if shift > 104:
                tiles[at + 1] = jnp.where(lane < shift, group, 0.0)
                group = jnp.where(lane >= shift, group, 0.0)
            tiles[at] = group if tiles[at] is None else tiles[at] + group
        for n in range(3):
            rows_out[zz, :, n * 128 : n * 128 + 128] = tiles[n].astype(BF16)

    pl.semaphore_wait(barrier, 47)

    def pair_copy(n):
        share = part32.at[(core + n) % 2, (zl + n // 2) % 2]
        return remote(share, pair_in.at[n], pair_send.at[n], pair_recv.at[n], quad(n))

    for n in (3, 2, 1):
        pair_copy(n).start()

    def rows_copy(k):
        to = (zh + k) % 4
        device = (x * 16 + to * 4 + y, orb)
        return remote(rows_out.at[to], rows_in.at[k], rows_send.at[k], rows_recv.at[k], device)

    @pl.loop(0, 4)
    def _(n):
        k = (n - zh + 4) % 4

        @pl.when(k != 0)
        def _():
            rows_copy(k).start()

    for n in (1, 2, 3):
        pair_copy(n).wait_recv()
    mine = (part32[core, zl % 2] + pair_in[1] + pair_in[2] + pair_in[3]).astype(BF16)
    part_out[...] = mine
    part_in[0] = mine

    def part_copy(k):
        return remote(part_out, part_in.at[k], part_send.at[k], part_recv.at[k], column(k))

    @pl.loop(0, 16)
    def _(n):
        k = column_to(n)

        @pl.when(k != 0)
        def _():
            part_copy(k).start()

    rows_in[0] = rows_out[zh]

    @pl.loop(1, 4)
    def _(k):
        rows_copy(k).wait_recv()

    for k in range(4):
        for n in range(3):
            rows32[n * 64 + k * 16 : n * 64 + k * 16 + 16, :] = rows_in[k, :, n * 128 : n * 128 + 128].astype(F32)
    for xx in range(4):
        t = [rows32[pl.ds(n * 64 + xx, 16, stride=4), :] for n in range(3)]
        owners = (
            t[0],
            jnp.where(lane < 32, pltpu.roll(t[0], 32, 1), pltpu.roll(t[1], 32, 1)),
            jnp.where(lane < 64, pltpu.roll(t[1], 64, 1), pltpu.roll(t[2], 64, 1)),
            pltpu.roll(t[2], 96, 1),
        )
        for yy in range(4):
            turn_out[xx * 4 + yy] = owners[yy].astype(BF16)

    def turn_copy(k):
        to = ((x + k // 4) % 4) * 4 + (y + k % 4) % 4
        return remote(turn_out.at[to], turn_in.at[k], turn_send.at[k], turn_recv.at[k], plane(k))

    @pl.loop(0, 16)
    def _(n):
        k = plane_to(n)

        @pl.when(k != 0)
        def _():
            turn_copy(k).start()

    turn_in[0] = turn_out[x * 4 + y]

    @pl.loop(1, 16)
    def _(k):
        part_copy(k).wait_recv()

    for h in range(4):
        for p in range(2):
            total = part_in[(4 * h + zl - p + 16) % 16].astype(F32) + part_in[(4 * h + zl - p + 14) % 16].astype(F32)
            sum32[h * 16 + p * 8 : h * 16 + p * 8 + 8, :] = total
    piece = [sum32[pl.ds(j, 16, stride=4), :] for j in range(4)]
    one, two, three = pltpu.roll(piece[1], 72, 1), pltpu.roll(piece[2], 16, 1), pltpu.roll(piece[3], 88, 1)
    left = (piece[0] + jnp.where(lane >= 72, one, 0.0)).astype(BF16)
    middle = (jnp.where(lane < 16, one, 0.0) + two + jnp.where(lane >= 88, three, 0.0)).astype(BF16)
    right = jnp.where(lane < 32, three, 0.0).astype(BF16)
    for n, tile in enumerate((left, middle, right)):
        block_out[:, n * 128 : n * 128 + 128] = tile
        gathered[core, 0, :, n * 128 : n * 128 + 128] = tile

    origin = vec // 16 + vec % 4 == 0

    def block_copy(n, source):
        there = gathered.at[source, n // 2]
        return remote(block_out, there, block_send.at[n], block_recv.at[source, n // 2], chips(n))

    def share_copy(n, source):
        there = gathered.at[source, pl.ds(n * 8, 8)]
        return remote(there, there, share_send.at[n], share_recv.at[n], sibling)

    first_k = plane_to(0)

    @pl.when(first_k != 0)
    def _():
        block_copy(2 * first_k + 1 - core, core).start()
        block_copy(2 * first_k + core, core).start()

    @pl.when(first_k == 0)
    def _():
        block_copy(1, core).start()

    @pl.loop(1, 16)
    def _(n):
        k = plane_to(n)

        @pl.when(k != 0)
        def _():
            block_copy(2 * k, core).start()

    @pl.loop(1, 16)
    def _(k):
        part_copy(k).wait_send()

    @pl.loop(1, 4)
    def _(k):
        rows_copy(k).wait_send()

    for n in (1, 2, 3):
        pair_copy(n).wait_send()

    @pl.when(jnp.logical_not(origin))
    def _():
        for n in range(2):

            @pl.loop(n * 8 + 1 - n, n * 8 + 8)
            def _(k):
                block_copy(2 * k, core).wait_recv()

            share_copy(n, core).start()

    @pl.loop(1, 16)
    def _(k):
        turn_copy(k).wait_recv()

    own = turn_in[...].reshape(256, 128).astype(F32).T[0:96].astype(BF16)

    @pl.when(origin)
    def _():
        @pl.loop(1, 16)
        def _(k):
            block_copy(2 * k, core).wait_recv()
            block_copy(2 * k, 1 - core).wait_recv()

        block_copy(1, 1 - core).wait_recv()

    @pl.when(jnp.logical_not(origin))
    def _():
        for n in range(2):
            share_copy(n, 1 - core).wait_recv()

    first = jnp.dot(own, gathered[0].reshape(256, 384), preferred_element_type=F32)
    second = jnp.dot(own, gathered[1].reshape(256, 384), preferred_element_type=F32)
    lane = lax.broadcasted_iota(jnp.int32, (96, 128), 1)
    a, b, c = (pltpu.roll(second[:, n * 128 : n * 128 + 128], 32, 1) for n in range(3))
    tiles = (
        first[:, 0:128],
        first[:, 128:256],
        first[:, 256:384] + jnp.where(lane >= 32, a, 0.0),
        jnp.where(lane < 32, a, b),
        jnp.where(lane < 32, b, c),
    )
    for n, tile in enumerate(tiles):
        width = min(128, 576 - n * 128)
        tile = tile[:, 0:width]
        out[:, :, n * 128 : n * 128 + width] = tile.reshape(4, 24, width)

    @pl.when(origin)
    def _():
        block_copy(1, core).wait_send()

    @pl.when(jnp.logical_not(origin))
    def _():
        block_copy(2 * first_k + 1, core).wait_send()
        for n in range(2):
            share_copy(n, core).wait_send()


    @pl.loop(1, 16)
    def _(k):
        turn_copy(k).wait_send()
        block_copy(2 * k, core).wait_send()


def fock_kernel(ints, density, out, fock, split, out_sem):
    copy = pltpu.make_async_copy(ints, out, out_sem)
    copy.start()
    tile = ints[...].reshape(96, 576)
    high = tile.astype(BF16)
    split[0:96, :] = high
    split[96:128, :] = jnp.zeros((32, 576), BF16)
    split[128:224, :] = (tile - high.astype(F32)).astype(BF16)

    pairs = lax.dot_general(density[...], split[...], NT, preferred_element_type=F32)
    pairs = pairs[:, 0:96] + pairs[:, 128:224]
    row = lax.broadcasted_iota(jnp.int32, (576, 96), 0) % 24
    col = lax.broadcasted_iota(jnp.int32, (576, 96), 1) % 24
    kept = jnp.where(row == col, pairs, 0.0).reshape(24, 24, 96).sum(axis=1)
    pick = lax.broadcasted_iota(jnp.int32, (4, 96), 0) == lax.broadcasted_iota(jnp.int32, (4, 96), 1) // 24
    fock[...] = lax.dot_general(
        pick.astype(F32), kept, NT, precision=lax.Precision.HIGHEST, preferred_element_type=F32
    )
    copy.wait()


def shards(cholesky, active_coeff, pair_density):
    vmem = pl.BlockSpec(memory_space=pltpu.VMEM)
    hbm = pl.BlockSpec(memory_space=pltpu.HBM)
    dma = pltpu.SemaphoreType.DMA
    ints = pl.pallas_call(
        kernel,
        name="half_active_fock",
        out_shape=jax.ShapeDtypeStruct((4, 24, 576), F32),
        in_specs=[hbm, hbm],
        out_specs=vmem,
        scratch_shapes=[
            pltpu.VMEM((4, 256, 2048), BF16),
            pltpu.VMEM((24, 2048), BF16),
            pltpu.VMEM((48, 128), F32),
            pltpu.VMEM((1024, 128), F32),
            pltpu.VMEM((4, 16, 384), BF16),
            pltpu.VMEM((4, 16, 384), BF16),
            pltpu.VMEM((192, 128), F32),
            pltpu.VMEM((16, 16, 128), BF16),
            pltpu.VMEM((16, 16, 128), BF16),
            pltpu.VMEM((2, 2, 8, 128), F32),
            pltpu.VMEM((4, 8, 128), F32),
            pltpu.VMEM((8, 128), BF16),
            pltpu.VMEM((16, 8, 128), BF16),
            pltpu.VMEM((64, 128), F32),
            pltpu.VMEM((16, 384), BF16),
            pltpu.VMEM((2, 16, 16, 384), BF16),
            dma((len(CUTS) - 1,)), dma, dma((4,)), dma((4,)), dma((4,)), dma((4,)), dma((16,)), dma((16,)),
            dma((16,)), dma((16,)), dma((32,)), dma((2, 16)), dma((2,)), dma((2,)),
        ],
        compiler_params=pltpu.CompilerParams(
            collective_id=0, has_side_effects=True, vmem_limit_bytes=16 * 2**20
        ),
    )(*(pltpu.with_memory_space_constraint(array, pltpu.HBM) for array in (cholesky, active_coeff.T)))
    return pl.pallas_call(
        fock_kernel,
        name="fock",
        out_shape=(jax.ShapeDtypeStruct((4, 24, 576), F32), jax.ShapeDtypeStruct((4, 24), F32)),
        in_specs=[vmem, vmem],
        out_specs=(hbm, vmem),
        scratch_shapes=[pltpu.VMEM((224, 576), BF16), dma],
        compiler_params=pltpu.CompilerParams(vmem_limit_bytes=16 * 2**20),
    )(ints, pair_density.reshape(576, 576))


def solution(mesh):
    return jax.shard_map(
        shards,
        mesh=mesh,
        in_specs=(P("vec", "orb", None), P(), P()),
        out_specs=(P(("orb", "vec"), None, None), P(("orb", "vec"), None)),
        check_vma=False,
    )
```

```python
import jax
import jax.numpy as jnp
from jax import lax
from jax.experimental import pallas as pl
from jax.experimental.pallas import tpu as pltpu
from jax.sharding import PartitionSpec as P

MESH = pl.DeviceIdType.MESH
F32 = jnp.float32
BF16 = jnp.bfloat16
NT = (((1,), (1,)), ((), ()))

CUTS = (0, 512, 1024, 1536, 1792, 2048)


def kernel(
    chol, coeff_h, out,
    chol_v, coeff_t, coeff_blk, half32, rows_out, rows_in, rows32,
    turn_out, turn_in, part32, pair_in, part_out, part_in, sum32, block_out, gathered,
    chol_sem, coeff_sem, pair_send, pair_recv, rows_send, rows_recv, part_send, part_recv,
    turn_send, turn_recv, block_send, block_recv, share_send, share_recv,
):
    vec, orb = lax.axis_index("vec"), lax.axis_index("orb")
    x, zh, y = vec // 16, (vec // 4) % 4, vec % 4
    zl, core = orb // 2, orb % 2

    def plane(k):
        return (((x + k // 4) % 4) * 16 + zh * 4 + (y + k % 4) % 4, orb)

    def column(k):
        to = (zh * 4 + zl + k) % 16
        return (x * 16 + (to // 4) * 4 + y, (to % 4) * 2 + core)

    def column_to(z):
        return (z - zh * 4 - zl + 16) % 16

    def plane_to(n):
        return ((n // 4 - x + 4) % 4) * 4 + (n % 4 - y + 4) % 4

    sibling = (vec, zl * 2 + 1 - core)

    def chips(n):
        vec_to, _ = plane(n // 2)
        return (vec_to, zl * 2 + (core + n) % 2)

    def quad(n):
        return (vec, ((zl // 2) * 2 + (zl + n // 2) % 2) * 2 + (core + n) % 2)

    def remote(src, dst, send, recv, device):
        return pltpu.make_async_remote_copy(
            src_ref=src, dst_ref=dst, send_sem=send, recv_sem=recv, device_id=device, device_id_type=MESH
        )

    def fetch(n):
        piece = (slice(None), slice(None), pl.ds(CUTS[n], CUTS[n + 1] - CUTS[n]))
        return pltpu.make_async_copy(chol.at[piece], chol_v.at[piece], chol_sem.at[n])

    coeff_copy = pltpu.make_async_copy(coeff_h, coeff_t, coeff_sem)
    coeff_copy.start()
    for n in range(len(CUTS) - 1):
        fetch(n).start()

    barrier = pltpu.get_barrier_semaphore()

    @pl.loop(0, 16, unroll=True)
    def _(n):
        k = column_to(n)

        @pl.when(k != 0)
        def _():
            pl.semaphore_signal(barrier, inc=1, device_id=column(k), device_id_type=MESH)

    pl.semaphore_signal(barrier, inc=1, device_id=sibling, device_id_type=MESH)
    pl.semaphore_signal(barrier, inc=1, device_id=quad(3), device_id_type=MESH)

    @pl.loop(0, 16, unroll=True)
    def _(n):
        k = plane_to(n)

        @pl.when(k != 0)
        def _():
            pl.semaphore_signal(barrier, inc=1, device_id=chips(2 * k + 1 - core), device_id_type=MESH)
            pl.semaphore_signal(barrier, inc=1, device_id=chips(2 * k + core), device_id_type=MESH)

    coeff_copy.wait()
    for n in range(2):
        lanes = pl.ds(pl.multiple_of(orb * 256 + n * 128, 128), 128)
        coeff_blk[n * 24 : n * 24 + 24, :] = coeff_t[:, lanes].astype(F32)
    coeff_rows = jnp.concatenate(
        [
            jnp.concatenate([coeff_blk[pl.ds(n * 24 + k, 8, stride=3), :] for k in range(3)], axis=0)
            for n in range(2)
        ],
        axis=1,
    ).astype(BF16)

    turned = None
    half32[...] = jnp.zeros_like(half32)
    for n in range(len(CUTS) - 1):
        fetch(n).wait()
        columns = slice(CUTS[n], CUTS[n + 1])
        term = lax.dot_general(
            coeff_t[:, columns],
            chol_v[:, :, columns].reshape(1024, -1),
            NT,
            preferred_element_type=F32,
        )
        turned = turned + term if n else term
    turned = turned.astype(BF16)
    stacked = jnp.concatenate([turned[:, q * 256 : q * 256 + 256] for q in range(4)], axis=0)
    part = lax.dot_general(coeff_rows, stacked, NT, preferred_element_type=F32)
    part = jnp.concatenate([part, jnp.zeros((24, 32), F32)], axis=1)
    lane8 = lax.broadcasted_iota(jnp.int32, (8, 128), 1)
    for q in range(4):
        packed = jnp.zeros((8, 128), F32)
        for k in range(3):
            piece = part[k * 8 : k * 8 + 8]
            shift = (24 * (k - q)) % 128
            piece = pltpu.roll(piece, shift, 1) if shift else piece
            packed = jnp.where((lane8 >= 24 * k) & (lane8 < 24 * k + 24), piece, packed)
        at = (q % 2) * 4
        part32[0, q // 2, at : at + 4, :] = packed[0:4]
        part32[1, q // 2, at : at + 4, :] = packed[4:8]

    half32[:, 0:24] = turned.astype(F32).T

    lane = lax.broadcasted_iota(jnp.int32, (16, 128), 1)
    for zz in range(4):
        tiles = [None] * 3
        for n in range(16):
            at, shift = divmod(24 * n, 128)
            group = half32[pl.ds(zz * 16 + n, 16, stride=64), :]
            group = pltpu.roll(group, shift, 1) if shift else group
            if shift > 104:
                tiles[at + 1] = jnp.where(lane < shift, group, 0.0)
                group = jnp.where(lane >= shift, group, 0.0)
            tiles[at] = group if tiles[at] is None else tiles[at] + group
        for n in range(3):
            rows_out[zz, :, n * 128 : n * 128 + 128] = tiles[n].astype(BF16)

    pl.semaphore_wait(barrier, 47)

    def pair_copy(n):
        share = part32.at[(core + n) % 2, (zl + n // 2) % 2]
        return remote(share, pair_in.at[n], pair_send.at[n], pair_recv.at[n], quad(n))

    for n in (3, 2, 1):
        pair_copy(n).start()

    def rows_copy(k):
        to = (zh + k) % 4
        device = (x * 16 + to * 4 + y, orb)
        return remote(rows_out.at[to], rows_in.at[k], rows_send.at[k], rows_recv.at[k], device)

    @pl.loop(0, 4, unroll=True)
    def _(n):
        k = (n - zh + 4) % 4

        @pl.when(k != 0)
        def _():
            rows_copy(k).start()

    for n in (1, 2, 3):
        pair_copy(n).wait_recv()
    mine = (part32[core, zl % 2] + pair_in[1] + pair_in[2] + pair_in[3]).astype(BF16)
    part_out[...] = mine
    part_in[0] = mine

    def part_copy(k):
        return remote(part_out, part_in.at[k], part_send.at[k], part_recv.at[k], column(k))

    @pl.loop(0, 16, unroll=True)
    def _(n):
        k = column_to(n)

        @pl.when(k != 0)
        def _():
            part_copy(k).start()

    rows_in[0] = rows_out[zh]

    @pl.loop(1, 4, unroll=True)
    def _(k):
        rows_copy(k).wait_recv()

    for k in range(4):
        for n in range(3):
            rows32[n * 64 + k * 16 : n * 64 + k * 16 + 16, :] = rows_in[k, :, n * 128 : n * 128 + 128].astype(F32)
    for xx in range(4):
        t = [rows32[pl.ds(n * 64 + xx, 16, stride=4), :] for n in range(3)]
        owners = (
            t[0],
            jnp.where(lane < 32, pltpu.roll(t[0], 32, 1), pltpu.roll(t[1], 32, 1)),
            jnp.where(lane < 64, pltpu.roll(t[1], 64, 1), pltpu.roll(t[2], 64, 1)),
            pltpu.roll(t[2], 96, 1),
        )
        for yy in range(4):
            turn_out[xx * 4 + yy] = owners[yy].astype(BF16)

    def turn_copy(k):
        to = ((x + k // 4) % 4) * 4 + (y + k % 4) % 4
        return remote(turn_out.at[to], turn_in.at[k], turn_send.at[k], turn_recv.at[k], plane(k))

    @pl.loop(0, 16, unroll=True)
    def _(n):
        k = plane_to(n)

        @pl.when(k != 0)
        def _():
            turn_copy(k).start()

    turn_in[0] = turn_out[x * 4 + y]

    @pl.loop(1, 16, unroll=True)
    def _(k):
        part_copy(k).wait_recv()

    for h in range(4):
        for p in range(2):
            total = part_in[(4 * h + zl - p + 16) % 16].astype(F32) + part_in[(4 * h + zl - p + 14) % 16].astype(F32)
            sum32[h * 16 + p * 8 : h * 16 + p * 8 + 8, :] = total
    piece = [sum32[pl.ds(j, 16, stride=4), :] for j in range(4)]
    one, two, three = pltpu.roll(piece[1], 72, 1), pltpu.roll(piece[2], 16, 1), pltpu.roll(piece[3], 88, 1)
    left = (piece[0] + jnp.where(lane >= 72, one, 0.0)).astype(BF16)
    middle = (jnp.where(lane < 16, one, 0.0) + two + jnp.where(lane >= 88, three, 0.0)).astype(BF16)
    right = jnp.where(lane < 32, three, 0.0).astype(BF16)
    for n, tile in enumerate((left, middle, right)):
        block_out[:, n * 128 : n * 128 + 128] = tile
        gathered[core, 0, :, n * 128 : n * 128 + 128] = tile

    origin = vec // 16 + vec % 4 == 0

    def block_copy(n, source):
        there = gathered.at[source, n // 2]
        return remote(block_out, there, block_send.at[n], block_recv.at[source, n // 2], chips(n))

    def share_copy(n, source):
        there = gathered.at[source, pl.ds(n * 8, 8)]
        return remote(there, there, share_send.at[n], share_recv.at[n], sibling)

    first_k = plane_to(0)

    @pl.when(first_k != 0)
    def _():
        block_copy(2 * first_k + 1 - core, core).start()
        block_copy(2 * first_k + core, core).start()

    @pl.when(first_k == 0)
    def _():
        block_copy(1, core).start()

    @pl.loop(1, 16, unroll=True)
    def _(n):
        k = plane_to(n)

        @pl.when(k != 0)
        def _():
            block_copy(2 * k, core).start()

    @pl.loop(1, 16, unroll=True)
    def _(k):
        part_copy(k).wait_send()

    @pl.loop(1, 4, unroll=True)
    def _(k):
        rows_copy(k).wait_send()

    for n in (1, 2, 3):
        pair_copy(n).wait_send()

    @pl.when(jnp.logical_not(origin))
    def _():
        for n in range(2):

            @pl.loop(n * 8 + 1 - n, n * 8 + 8, unroll=True)
            def _(k):
                block_copy(2 * k, core).wait_recv()

            share_copy(n, core).start()

    @pl.loop(1, 16, unroll=True)
    def _(k):
        turn_copy(k).wait_recv()

    own = turn_in[...].reshape(256, 128).astype(F32).T[0:96].astype(BF16)

    @pl.when(origin)
    def _():
        @pl.loop(1, 16, unroll=True)
        def _(k):
            block_copy(2 * k, core).wait_recv()
            block_copy(2 * k, 1 - core).wait_recv()

        block_copy(1, 1 - core).wait_recv()

    @pl.when(jnp.logical_not(origin))
    def _():
        for n in range(2):
            share_copy(n, 1 - core).wait_recv()

    first = jnp.dot(own, gathered[0].reshape(256, 384), preferred_element_type=F32)
    second = jnp.dot(own, gathered[1].reshape(256, 384), preferred_element_type=F32)
    lane = lax.broadcasted_iota(jnp.int32, (96, 128), 1)
    a, b, c = (pltpu.roll(second[:, n * 128 : n * 128 + 128], 32, 1) for n in range(3))
    tiles = (
        first[:, 0:128],
        first[:, 128:256],
        first[:, 256:384] + jnp.where(lane >= 32, a, 0.0),
        jnp.where(lane < 32, a, b),
        jnp.where(lane < 32, b, c),
    )
    for n, tile in enumerate(tiles):
        width = min(128, 576 - n * 128)
        tile = tile[:, 0:width]
        out[:, :, n * 128 : n * 128 + width] = tile.reshape(4, 24, width)

    @pl.when(origin)
    def _():
        block_copy(1, core).wait_send()

    @pl.when(jnp.logical_not(origin))
    def _():
        block_copy(2 * first_k + 1, core).wait_send()
        for n in range(2):
            share_copy(n, core).wait_send()


    @pl.loop(1, 16, unroll=True)
    def _(k):
        turn_copy(k).wait_send()
        block_copy(2 * k, core).wait_send()


def fock_kernel(ints, density, out, fock, split, out_sem):
    copy = pltpu.make_async_copy(ints, out, out_sem)
    copy.start()
    tile = ints[...].reshape(96, 576)
    high = tile.astype(BF16)
    split[0:96, :] = high
    split[96:128, :] = jnp.zeros((32, 576), BF16)
    split[128:224, :] = (tile - high.astype(F32)).astype(BF16)

    pairs = lax.dot_general(density[...], split[...], NT, preferred_element_type=F32)
    pairs = pairs[:, 0:96] + pairs[:, 128:224]
    row = lax.broadcasted_iota(jnp.int32, (576, 96), 0) % 24
    col = lax.broadcasted_iota(jnp.int32, (576, 96), 1) % 24
    kept = jnp.where(row == col, pairs, 0.0).reshape(24, 24, 96).sum(axis=1)
    pick = lax.broadcasted_iota(jnp.int32, (4, 96), 0) == lax.broadcasted_iota(jnp.int32, (4, 96), 1) // 24
    fock[...] = lax.dot_general(
        pick.astype(F32), kept, NT, precision=lax.Precision.HIGHEST, preferred_element_type=F32
    )
    copy.wait()


def shards(cholesky, active_coeff, pair_density):
    vmem = pl.BlockSpec(memory_space=pltpu.VMEM)
    hbm = pl.BlockSpec(memory_space=pltpu.HBM)
    dma = pltpu.SemaphoreType.DMA
    ints = pl.pallas_call(
        kernel,
        name="half_active_fock",
        out_shape=jax.ShapeDtypeStruct((4, 24, 576), F32),
        in_specs=[hbm, hbm],
        out_specs=vmem,
        scratch_shapes=[
            pltpu.VMEM((4, 256, 2048), BF16),
            pltpu.VMEM((24, 2048), BF16),
            pltpu.VMEM((48, 128), F32),
            pltpu.VMEM((1024, 128), F32),
            pltpu.VMEM((4, 16, 384), BF16),
            pltpu.VMEM((4, 16, 384), BF16),
            pltpu.VMEM((192, 128), F32),
            pltpu.VMEM((16, 16, 128), BF16),
            pltpu.VMEM((16, 16, 128), BF16),
            pltpu.VMEM((2, 2, 8, 128), F32),
            pltpu.VMEM((4, 8, 128), F32),
            pltpu.VMEM((8, 128), BF16),
            pltpu.VMEM((16, 8, 128), BF16),
            pltpu.VMEM((64, 128), F32),
            pltpu.VMEM((16, 384), BF16),
            pltpu.VMEM((2, 16, 16, 384), BF16),
            dma((len(CUTS) - 1,)), dma, dma((4,)), dma((4,)), dma((4,)), dma((4,)), dma((16,)), dma((16,)),
            dma((16,)), dma((16,)), dma((32,)), dma((2, 16)), dma((2,)), dma((2,)),
        ],
        compiler_params=pltpu.CompilerParams(
            collective_id=0, has_side_effects=True, vmem_limit_bytes=16 * 2**20
        ),
    )(*(pltpu.with_memory_space_constraint(array, pltpu.HBM) for array in (cholesky, active_coeff.T)))
    return pl.pallas_call(
        fock_kernel,
        name="fock",
        out_shape=(jax.ShapeDtypeStruct((4, 24, 576), F32), jax.ShapeDtypeStruct((4, 24), F32)),
        in_specs=[vmem, vmem],
        out_specs=(hbm, vmem),
        scratch_shapes=[pltpu.VMEM((224, 576), BF16), dma],
        compiler_params=pltpu.CompilerParams(vmem_limit_bytes=16 * 2**20),
    )(ints, pair_density.reshape(576, 576))


def solution(mesh):
    return jax.shard_map(
        shards,
        mesh=mesh,
        in_specs=(P("vec", "orb", None), P(), P()),
        out_specs=(P(("orb", "vec"), None, None), P(("orb", "vec"), None)),
        check_vma=False,
    )
```

```python
import jax
import jax.numpy as jnp
from jax import lax
from jax.experimental import pallas as pl
from jax.experimental.pallas import tpu as pltpu
from jax.sharding import PartitionSpec as P

MESH = pl.DeviceIdType.MESH
F32 = jnp.float32
BF16 = jnp.bfloat16
NT = (((1,), (1,)), ((), ()))

CUTS = (0, 512, 1024, 1536, 1792, 2048)


def kernel(
    chol, coeff_h, out,
    chol_v, coeff_t, coeff_blk, half32, rows_out, rows_in, rows32,
    turn_out, turn_in, part32, pair_in, part_out, part_in, sum32, block_out, gathered,
    chol_sem, coeff_sem, pair_send, pair_recv, rows_send, rows_recv, part_send, part_recv,
    turn_send, turn_recv, block_send, block_recv, share_send, share_recv,
):
    vec, orb = lax.axis_index("vec"), lax.axis_index("orb")
    x, zh, y = vec // 16, (vec // 4) % 4, vec % 4
    zl, core = orb // 2, orb % 2

    def plane(k):
        return (((x + k // 4) % 4) * 16 + zh * 4 + (y + k % 4) % 4, orb)

    def column(k):
        to = (zh * 4 + zl + k) % 16
        return (x * 16 + (to // 4) * 4 + y, (to % 4) * 2 + core)

    def column_to(z):
        return (z - zh * 4 - zl + 16) % 16

    def plane_to(n):
        return ((n // 4 - x + 4) % 4) * 4 + (n % 4 - y + 4) % 4

    sibling = (vec, zl * 2 + 1 - core)

    def chips(n):
        vec_to, _ = plane(n // 2)
        return (vec_to, zl * 2 + (core + n) % 2)

    def quad(n):
        return (vec, ((zl // 2) * 2 + (zl + n // 2) % 2) * 2 + (core + n) % 2)

    def remote(src, dst, send, recv, device):
        return pltpu.make_async_remote_copy(
            src_ref=src, dst_ref=dst, send_sem=send, recv_sem=recv, device_id=device, device_id_type=MESH
        )

    def fetch(n):
        piece = (slice(None), slice(None), pl.ds(CUTS[n], CUTS[n + 1] - CUTS[n]))
        return pltpu.make_async_copy(chol.at[piece], chol_v.at[piece], chol_sem.at[n])

    coeff_copy = pltpu.make_async_copy(coeff_h, coeff_t, coeff_sem)
    coeff_copy.start()
    for n in range(len(CUTS) - 1):
        fetch(n).start()

    barrier = pltpu.get_barrier_semaphore()

    @pl.loop(0, 16, unroll=True)
    def _(n):
        k = column_to(n)

        @pl.when(k != 0)
        def _():
            pl.semaphore_signal(barrier, inc=1, device_id=column(k), device_id_type=MESH)

    pl.semaphore_signal(barrier, inc=1, device_id=sibling, device_id_type=MESH)
    pl.semaphore_signal(barrier, inc=1, device_id=quad(3), device_id_type=MESH)

    @pl.loop(0, 16, unroll=True)
    def _(n):
        k = plane_to(n)

        @pl.when(k != 0)
        def _():
            pl.semaphore_signal(barrier, inc=1, device_id=chips(2 * k + 1 - core), device_id_type=MESH)
            pl.semaphore_signal(barrier, inc=1, device_id=chips(2 * k + core), device_id_type=MESH)

    coeff_copy.wait()
    for n in range(2):
        lanes = pl.ds(pl.multiple_of(orb * 256 + n * 128, 128), 128)
        coeff_blk[n * 24 : n * 24 + 24, :] = coeff_t[:, lanes].astype(F32)
    coeff_rows = jnp.concatenate(
        [
            jnp.concatenate([coeff_blk[pl.ds(n * 24 + k, 8, stride=3), :] for k in range(3)], axis=0)
            for n in range(2)
        ],
        axis=1,
    ).astype(BF16)

    turned = None
    half32[...] = jnp.zeros_like(half32)
    for n in range(len(CUTS) - 1):
        fetch(n).wait()
        columns = slice(CUTS[n], CUTS[n + 1])
        term = lax.dot_general(
            coeff_t[:, columns],
            chol_v[:, :, columns].reshape(1024, -1),
            NT,
            preferred_element_type=F32,
        )
        turned = turned + term if n else term
    turned = turned.astype(BF16)
    stacked = jnp.concatenate([turned[:, q * 256 : q * 256 + 256] for q in range(4)], axis=0)
    part = lax.dot_general(coeff_rows, stacked, NT, preferred_element_type=F32)
    part = jnp.concatenate([part, jnp.zeros((24, 32), F32)], axis=1)
    lane8 = lax.broadcasted_iota(jnp.int32, (8, 128), 1)
    for q in range(4):
        packed = jnp.zeros((8, 128), F32)
        for k in range(3):
            piece = part[k * 8 : k * 8 + 8]
            shift = (24 * (k - q)) % 128
            piece = pltpu.roll(piece, shift, 1) if shift else piece
            packed = jnp.where((lane8 >= 24 * k) & (lane8 < 24 * k + 24), piece, packed)
        at = (q % 2) * 4
        part32[0, q // 2, at : at + 4, :] = packed[0:4]
        part32[1, q // 2, at : at + 4, :] = packed[4:8]

    half32[:, 0:24] = turned.astype(F32).T

    lane = lax.broadcasted_iota(jnp.int32, (16, 128), 1)
    for zz in range(4):
        tiles = [None] * 3
        for n in range(16):
            at, shift = divmod(24 * n, 128)
            group = half32[pl.ds(zz * 16 + n, 16, stride=64), :]
            group = pltpu.roll(group, shift, 1) if shift else group
            if shift > 104:
                tiles[at + 1] = jnp.where(lane < shift, group, 0.0)
                group = jnp.where(lane >= shift, group, 0.0)
            tiles[at] = group if tiles[at] is None else tiles[at] + group
        for n in range(3):
            rows_out[zz, :, n * 128 : n * 128 + 128] = tiles[n].astype(BF16)

    pl.semaphore_wait(barrier, 47)

    def pair_copy(n):
        share = part32.at[(core + n) % 2, (zl + n // 2) % 2]
        return remote(share, pair_in.at[n], pair_send.at[n], pair_recv.at[n], quad(n))

    for n in (3, 2, 1):
        pair_copy(n).start()

    def rows_copy(k):
        to = (zh + k) % 4
        device = (x * 16 + to * 4 + y, orb)
        return remote(rows_out.at[to], rows_in.at[k], rows_send.at[k], rows_recv.at[k], device)

    @pl.loop(0, 4, unroll=True)
    def _(n):
        k = (n - zh + 4) % 4

        @pl.when(k != 0)
        def _():
            rows_copy(k).start()

    for n in (1, 2, 3):
        pair_copy(n).wait_recv()
    mine = (part32[core, zl % 2] + pair_in[1] + pair_in[2] + pair_in[3]).astype(BF16)
    part_out[...] = mine
    part_in[0] = mine

    def part_copy(k):
        return remote(part_out, part_in.at[k], part_send.at[k], part_recv.at[k], column(k))

    @pl.loop(0, 16, unroll=True)
    def _(n):
        k = column_to(n)

        @pl.when(k != 0)
        def _():
            part_copy(k).start()

    rows_in[0] = rows_out[zh]

    @pl.loop(1, 4, unroll=True)
    def _(k):
        rows_copy(k).wait_recv()

    for k in range(4):
        for n in range(3):
            rows32[n * 64 + k * 16 : n * 64 + k * 16 + 16, :] = rows_in[k, :, n * 128 : n * 128 + 128].astype(F32)
    for xx in range(4):
        t = [rows32[pl.ds(n * 64 + xx, 16, stride=4), :] for n in range(3)]
        owners = (
            t[0],
            jnp.where(lane < 32, pltpu.roll(t[0], 32, 1), pltpu.roll(t[1], 32, 1)),
            jnp.where(lane < 64, pltpu.roll(t[1], 64, 1), pltpu.roll(t[2], 64, 1)),
            pltpu.roll(t[2], 96, 1),
        )
        for yy in range(4):
            turn_out[xx * 4 + yy] = owners[yy].astype(BF16)

    def turn_copy(k):
        to = ((x + k // 4) % 4) * 4 + (y + k % 4) % 4
        return remote(turn_out.at[to], turn_in.at[k], turn_send.at[k], turn_recv.at[k], plane(k))

    @pl.loop(0, 16, unroll=True)
    def _(n):
        k = plane_to(n)

        @pl.when(k != 0)
        def _():
            turn_copy(k).start()

    turn_in[0] = turn_out[x * 4 + y]

    @pl.loop(1, 16, unroll=True)
    def _(k):
        part_copy(k).wait_recv()

    for h in range(4):
        for p in range(2):
            total = part_in[(4 * h + zl - p + 16) % 16].astype(F32) + part_in[(4 * h + zl - p + 14) % 16].astype(F32)
            sum32[h * 16 + p * 8 : h * 16 + p * 8 + 8, :] = total
    piece = [sum32[pl.ds(j, 16, stride=4), :] for j in range(4)]
    one, two, three = pltpu.roll(piece[1], 72, 1), pltpu.roll(piece[2], 16, 1), pltpu.roll(piece[3], 88, 1)
    left = (piece[0] + jnp.where(lane >= 72, one, 0.0)).astype(BF16)
    middle = (jnp.where(lane < 16, one, 0.0) + two + jnp.where(lane >= 88, three, 0.0)).astype(BF16)
    right = jnp.where(lane < 32, three, 0.0).astype(BF16)
    for n, tile in enumerate((left, middle, right)):
        block_out[:, n * 128 : n * 128 + 128] = tile
        gathered[core, 0, :, n * 128 : n * 128 + 128] = tile

    origin = vec // 16 + vec % 4 == 0

    def block_copy(n, source):
        there = gathered.at[source, n // 2]
        return remote(block_out, there, block_send.at[n], block_recv.at[source, n // 2], chips(n))

    def share_copy(n, source):
        there = gathered.at[source, pl.ds(n * 4, 4)]
        return remote(there, there, share_send.at[n], share_recv.at[n], sibling)

    first_k = plane_to(0)

    @pl.when(first_k != 0)
    def _():
        block_copy(2 * first_k + 1 - core, core).start()
        block_copy(2 * first_k + core, core).start()

    @pl.when(first_k == 0)
    def _():
        block_copy(1, core).start()

    @pl.loop(1, 16, unroll=True)
    def _(n):
        k = plane_to(n)

        @pl.when(k != 0)
        def _():
            block_copy(2 * k, core).start()

    @pl.loop(1, 16, unroll=True)
    def _(k):
        part_copy(k).wait_send()

    @pl.loop(1, 4, unroll=True)
    def _(k):
        rows_copy(k).wait_send()

    for n in (1, 2, 3):
        pair_copy(n).wait_send()

    @pl.when(jnp.logical_not(origin))
    def _():
        for n in range(4):

            @pl.loop(max(n * 4, 1), n * 4 + 4, unroll=True)
            def _(k):
                block_copy(2 * k, core).wait_recv()

            share_copy(n, core).start()

    @pl.loop(1, 16, unroll=True)
    def _(k):
        turn_copy(k).wait_recv()

    own = turn_in[...].reshape(256, 128).astype(F32).T[0:96].astype(BF16)

    @pl.when(origin)
    def _():
        @pl.loop(1, 16, unroll=True)
        def _(k):
            block_copy(2 * k, core).wait_recv()
            block_copy(2 * k, 1 - core).wait_recv()

        block_copy(1, 1 - core).wait_recv()

    @pl.when(jnp.logical_not(origin))
    def _():
        for n in range(4):
            share_copy(n, 1 - core).wait_recv()

    first = jnp.dot(own, gathered[0].reshape(256, 384), preferred_element_type=F32)
    second = jnp.dot(own, gathered[1].reshape(256, 384), preferred_element_type=F32)
    lane = lax.broadcasted_iota(jnp.int32, (96, 128), 1)
    a, b, c = (pltpu.roll(second[:, n * 128 : n * 128 + 128], 32, 1) for n in range(3))
    tiles = (
        first[:, 0:128],
        first[:, 128:256],
        first[:, 256:384] + jnp.where(lane >= 32, a, 0.0),
        jnp.where(lane < 32, a, b),
        jnp.where(lane < 32, b, c),
    )
    for n, tile in enumerate(tiles):
        width = min(128, 576 - n * 128)
        tile = tile[:, 0:width]
        out[:, :, n * 128 : n * 128 + width] = tile.reshape(4, 24, width)

    @pl.when(origin)
    def _():
        block_copy(1, core).wait_send()

    @pl.when(jnp.logical_not(origin))
    def _():
        block_copy(2 * first_k + 1, core).wait_send()
        for n in range(4):
            share_copy(n, core).wait_send()


    @pl.loop(1, 16, unroll=True)
    def _(k):
        turn_copy(k).wait_send()
        block_copy(2 * k, core).wait_send()


def fock_kernel(ints, density, out, fock, split, out_sem):
    copy = pltpu.make_async_copy(ints, out, out_sem)
    copy.start()
    tile = ints[...].reshape(96, 576)
    high = tile.astype(BF16)
    split[0:96, :] = high
    split[96:128, :] = jnp.zeros((32, 576), BF16)
    split[128:224, :] = (tile - high.astype(F32)).astype(BF16)

    pairs = lax.dot_general(density[...], split[...], NT, preferred_element_type=F32)
    pairs = pairs[:, 0:96] + pairs[:, 128:224]
    row = lax.broadcasted_iota(jnp.int32, (576, 96), 0) % 24
    col = lax.broadcasted_iota(jnp.int32, (576, 96), 1) % 24
    kept = jnp.where(row == col, pairs, 0.0).reshape(24, 24, 96).sum(axis=1)
    pick = lax.broadcasted_iota(jnp.int32, (4, 96), 0) == lax.broadcasted_iota(jnp.int32, (4, 96), 1) // 24
    fock[...] = lax.dot_general(
        pick.astype(F32), kept, NT, precision=lax.Precision.HIGHEST, preferred_element_type=F32
    )
    copy.wait()


def shards(cholesky, active_coeff, pair_density):
    vmem = pl.BlockSpec(memory_space=pltpu.VMEM)
    hbm = pl.BlockSpec(memory_space=pltpu.HBM)
    dma = pltpu.SemaphoreType.DMA
    ints = pl.pallas_call(
        kernel,
        name="half_active_fock",
        out_shape=jax.ShapeDtypeStruct((4, 24, 576), F32),
        in_specs=[hbm, hbm],
        out_specs=vmem,
        scratch_shapes=[
            pltpu.VMEM((4, 256, 2048), BF16),
            pltpu.VMEM((24, 2048), BF16),
            pltpu.VMEM((48, 128), F32),
            pltpu.VMEM((1024, 128), F32),
            pltpu.VMEM((4, 16, 384), BF16),
            pltpu.VMEM((4, 16, 384), BF16),
            pltpu.VMEM((192, 128), F32),
            pltpu.VMEM((16, 16, 128), BF16),
            pltpu.VMEM((16, 16, 128), BF16),
            pltpu.VMEM((2, 2, 8, 128), F32),
            pltpu.VMEM((4, 8, 128), F32),
            pltpu.VMEM((8, 128), BF16),
            pltpu.VMEM((16, 8, 128), BF16),
            pltpu.VMEM((64, 128), F32),
            pltpu.VMEM((16, 384), BF16),
            pltpu.VMEM((2, 16, 16, 384), BF16),
            dma((len(CUTS) - 1,)), dma, dma((4,)), dma((4,)), dma((4,)), dma((4,)), dma((16,)), dma((16,)),
            dma((16,)), dma((16,)), dma((32,)), dma((2, 16)), dma((4,)), dma((4,)),
        ],
        compiler_params=pltpu.CompilerParams(
            collective_id=0, has_side_effects=True, vmem_limit_bytes=16 * 2**20
        ),
    )(*(pltpu.with_memory_space_constraint(array, pltpu.HBM) for array in (cholesky, active_coeff.T)))
    return pl.pallas_call(
        fock_kernel,
        name="fock",
        out_shape=(jax.ShapeDtypeStruct((4, 24, 576), F32), jax.ShapeDtypeStruct((4, 24), F32)),
        in_specs=[vmem, vmem],
        out_specs=(hbm, vmem),
        scratch_shapes=[pltpu.VMEM((224, 576), BF16), dma],
        compiler_params=pltpu.CompilerParams(vmem_limit_bytes=16 * 2**20),
    )(ints, pair_density.reshape(576, 576))


def solution(mesh):
    return jax.shard_map(
        shards,
        mesh=mesh,
        in_specs=(P("vec", "orb", None), P(), P()),
        out_specs=(P(("orb", "vec"), None, None), P(("orb", "vec"), None)),
        check_vma=False,
    )
```
